256 devices in a mesh: dp: 64 (over z_hi, x, y, core), mp: 4 (over z_lo).
Axes of the slice: x: 4, y: 4, z: 8 (z_hi: 2, z_lo: 4; z = z_hi * 4 + z_lo), core: 2. Of those that a mesh axis runs over, the one named last changes fastest.
Arguments:
- hidden_acts: bfloat16 [98304, 1024], P('dp'), may hold values from -7168 to 7168
- out_grads: bfloat16 [98304, 8192], P('dp', 'mp'), may hold values from -6 to 6
- token_counts: int32 [64], P('dp'), may hold values from 1 to 1536, as said below
- down_weight: bfloat16 [1024, 8192], P(None, 'mp'), may hold values from -0.0625 to 0.0625
- owner_map: int32 [64], replicated, may hold values from 0 to 63, each once
- master: float32 [1024, 8192], P('dp', 'mp'), may hold values from -0.046875 to 0.046875
- moment1: float32 [1024, 8192], P('dp', 'mp'), may hold values from -6 to 6
- moment2: bfloat16 [1024, 8192], P('dp', 'mp'), may hold values from 0.099609375 to 10
Outputs:
- master_new: float32 [1024, 8192], P('dp', 'mp')
- moment1_new: float32 [1024, 8192], P('dp', 'mp')
- moment2_new: bfloat16 [1024, 8192], P('dp', 'mp')
- weights_new: bfloat16 [1024, 8192], P(None, 'mp')
- input_grads: bfloat16 [98304, 1024], P('dp', 'mp')
The draws below stay inside these ranges and needn't reach their ends.
Inputs may be any that keep to these rules, and one draw needn't show every extreme that they name: `token_counts`: the last worker is always full; the others hold from about a third to all of their 1536 slots, rising along the workers.
All inputs are finite; a program needn't handle non-finite values.
Results may differ from the reference program's by a relative error of at most 0.0026.
Values may be sent and summed in bfloat16 or wider, within the bound.
No kernel may reach another device: no remote copies, remote signals or barrier semaphores. Data moves between devices by JAX's collectives and lax.ppermute only.
A program may use at most 128 MiB of HBM per device.

```python
import math
import jax
import jax.numpy as jnp
from jax import lax

D = 8192
TOK_DEV = 1536
HB = 1024
TOKENS = 98304
N_DP = 64


def draw_token_counts(key, part):
    workers = jnp.arange(N_DP, dtype=jnp.int32)
    lowest = TOK_DEV // 3
    base = lowest + workers * (TOK_DEV - lowest) // max(N_DP - 1, 1)
    jitter = jax.random.randint(jax.random.fold_in(key, 17), (N_DP,), 0, TOK_DEV // 8 + 1)
    counts = jnp.maximum(base - jitter, 1)
    return jnp.where(workers == N_DP - 1, TOK_DEV, counts).astype(jnp.int32)


def spiked(array, stream_key, source, target, parts, factor):
    owner, partner = [(jnp.arange(array.shape[position]) // (array.shape[position] // parts)).reshape([-1 if axis == position else 1 for axis in range(array.ndim)]) for position in (source, target)]
    chosen = jax.random.permutation(stream_key, parts)[partner]
    strong = (owner == chosen) | (owner == (partner + parts // 2) % parts)
    return jnp.where(strong, factor * array, array)


def levels(own_key, extent, pieces, least, high):
    gain = 1.0
    for position, shards_of in pieces:
        steps = jax.random.uniform(jax.random.fold_in(jax.random.fold_in(own_key, 6), position), (shards_of,), jnp.float32, least / len(pieces), high / len(pieces))
        gain = gain * jnp.repeat(jnp.exp(steps), extent[position] // shards_of).reshape((-1,) + (1,) * (len(extent) - 1 - position))
    return gain


def scatter_about(own_key, dims, width, limit, pieces=(), kind=jnp.bfloat16):
    result = width * jax.random.normal(own_key, dims, jnp.float32)
    if pieces:
        result = result * levels(own_key, dims, pieces, -0.22, 0.18)
    return jnp.clip(result, -limit, limit).astype(kind)


def bell_draw_with(key, extent, deviation, limit, pieces, heavy, kind=jnp.bfloat16):
    result = deviation * jax.random.normal(key, extent, jnp.float32)
    if pieces:
        result = result * levels(key, extent, pieces, -0.22, 0.18)
    return jnp.clip(spiked(result, jax.random.fold_in(key, 3), *heavy), -limit, limit).astype(kind)


def setup_inputs(seed: int = 0) -> dict:
    key_of = jax.random.split(jax.random.key(seed), 9)
    return {
        "hidden_acts": bell_draw_with(key_of[0], (TOKENS, HB), (N_DP + TOK_DEV // 4), 7168.0, ((0, 64),), (0, 1, 64, 4.0)),
        "out_grads": scatter_about(key_of[1], (TOKENS, D), 1.0, 6.0, ((0, 64), (1, 4))),
        "token_counts": draw_token_counts(jax.random.fold_in(key_of[8], 71), 0),
        "down_weight": scatter_about(key_of[3], (HB, D), D ** -0.5, 0.0625, ((1, 4),)),
        "owner_map": jax.random.permutation(key_of[4], N_DP).astype(jnp.int32),
        "master": scatter_about(key_of[5], (HB, D), 0.003, 0.046875, ((0, 64), (1, 4)), jnp.float32),
        "moment1": scatter_about(key_of[6], (HB, D), 1.0, 6.0, ((0, 64), (1, 4)), jnp.float32),
        "moment2": jnp.clip(jnp.exp(math.log(10.0) - 4.609084 * jax.random.uniform(key_of[7], (HB, D), jnp.float32) ** levels(key_of[7], (HB, D), ((0, 64), (1, 4)), -0.2, 0.2)), 0.099609375, 10.0).astype(jnp.bfloat16),
    }


beta_one = 0.9
beta_two = 0.95
learn_rate = 0.0003
epsilon = 1e-08
correct_one = 1.0 - 0.9 ** 50
correct_two = 1.0 - 0.95 ** 50

def reference(hidden_acts, out_grads, token_counts, down_weight, owner_map, master, moment1, moment2):
    block = HB // N_DP
    positions = jnp.arange(TOKENS, dtype=jnp.int32)
    worker_of = positions // TOK_DEV
    valid = positions % TOK_DEV < token_counts[worker_of]
    masked = jnp.where(valid[:, None], out_grads, jnp.zeros_like(out_grads))

    def accumulate(total_sum, worker):
        start = (worker * TOK_DEV).astype(jnp.int32)
        acts = lax.dynamic_slice_in_dim(hidden_acts, start, TOK_DEV, 0)
        grads = lax.dynamic_slice_in_dim(masked, start, TOK_DEV, 0)
        term = lax.dot_general(acts, grads, (((0,), (0,)), ((), ())), preferred_element_type=jnp.float32)
        term = lax.optimization_barrier(term.astype(jnp.bfloat16)).astype(jnp.float32)
        return (total_sum + term, None)
    summed, _ = lax.scan(accumulate, jnp.zeros((HB, D), jnp.float32), jnp.arange(N_DP, dtype=jnp.int32))
    total = jnp.sum(token_counts).astype(jnp.float32)
    grad = summed / total
    grad_slots = jnp.take(grad.reshape(N_DP, block, D), owner_map, axis=0).reshape(HB, D)
    moment1_new = beta_one * moment1 + (1.0 - beta_one) * grad_slots
    second = beta_two * moment2.astype(jnp.float32) + (1.0 - beta_two) * grad_slots * grad_slots
    moment2_new = second.astype(jnp.bfloat16)
    master_new = master - learn_rate * (moment1_new / correct_one) / (jnp.sqrt(second / correct_two) + epsilon)
    slot_weights = master_new.astype(jnp.bfloat16).reshape(N_DP, block, D)
    weights_new = jnp.zeros((N_DP, block, D), jnp.bfloat16).at[owner_map].set(slot_weights).reshape(HB, D)
    input_grads = lax.dot_general(masked, down_weight, (((1,), (1,)), ((), ())), preferred_element_type=jnp.float32).astype(jnp.bfloat16)
    return (master_new, moment1_new, moment2_new, weights_new, input_grads)
```

```python
import jax
import jax.numpy as jnp
from jax import lax
from jax.experimental import pallas as pl
from jax.experimental.pallas import tpu as pltpu
from jax.sharding import PartitionSpec as P

beta_one = 0.9
beta_two = 0.95
learn_rate = 0.0003
epsilon = 1e-08
correct_one = 1.0 - 0.9**50
correct_two = 1.0 - 0.95**50


ZH, X, Y, CORE = 2, 4, 4, 2
f32, bf16, f16 = jnp.float32, jnp.bfloat16, jnp.float16


def index_of(zh, x, y, core):
    return ((zh * X + x) * Y + y) * CORE + core


def move(value, to):
    pairs = [
        (index_of(z, x, y, c), index_of(*to(z, x, y, c)))
        for z in range(ZH)
        for x in range(X)
        for y in range(Y)
        for c in range(CORE)
    ]
    return lax.ppermute(value, "dp", pairs)


def to_core(value):
    return move(value, lambda z, x, y, c: (z, x, y, 1 - c))


def to_zh(value):
    return move(value, lambda z, x, y, c: (1 - z, x, y, c))


def shift(value, ring, by):
    if ring == "x":
        return move(value, lambda z, x, y, c: (z, (x + by) % X, y, c))
    return move(value, lambda z, x, y, c: (z, x, (y + by) % Y, c))


def pick(array, index):
    return array.at[index].get(mode="promise_in_bounds")


def place_blocks(halves, blocks, height, width):
    sizes = [[piece.shape[0] for piece in pieces] for pieces, _ in halves]
    pieces = [piece for group, _ in halves for piece in group]

    def kernel(*refs):
        tables, sources = refs[: len(halves)], list(refs[len(halves) : -2])
        out, sem = refs[-2], refs[-1]
        for part, (table, counts) in enumerate(zip(tables, sizes)):
            columns = pl.ds(part * width, width)
            base = 0
            for count in counts:
                source = sources.pop(0)

                def start(step, carry, source=source, base=base, table=table, columns=columns):
                    pltpu.make_async_copy(
                        source.at[step], out.at[table[base + step], :, columns], sem
                    ).start()
                    return carry

                lax.fori_loop(0, count, start, 0)
                base += count
        pltpu.make_async_copy(out, out, sem).wait()

    return pl.pallas_call(
        kernel,
        out_shape=jax.ShapeDtypeStruct((blocks, height, width * len(halves)), bf16),
        in_specs=[pl.BlockSpec(memory_space=pltpu.SMEM)] * len(halves)
        + [pl.BlockSpec(memory_space=pl.ANY)] * len(pieces),
        out_specs=pl.BlockSpec(memory_space=pl.ANY),
        scratch_shapes=[pltpu.SemaphoreType.DMA],
    )(*[table for _, table in halves], *pieces)


def per_device(
    hidden_acts, out_grads, token_counts, down_weight, owner_map, master, moment1, moment2
):
    rows, columns = out_grads.shape
    hidden = hidden_acts.shape[1]
    workers = ZH * X * Y * CORE
    block = hidden // workers
    half = columns // 2
    me = lax.axis_index("dp")
    my_core, my_y, my_x, my_zh = me % 2, (me // 2) % 4, (me // 8) % 4, me // 32
    my_mp = lax.axis_index("mp")
    shares = hidden // 4

    valid = lax.iota(jnp.int32, rows) < token_counts[0]
    masked = jnp.where(valid[:, None], out_grads, jnp.zeros_like(out_grads))

    total = to_core(token_counts) + token_counts
    for ring in ("x", "y"):
        total = total + shift(total, ring, 1)
        total = total + shift(total, ring, 2)
    total = total + to_zh(total)
    total = total[0].astype(f32)

    order = jnp.arange(workers, dtype=jnp.int32)
    rel_core, rel_1, rel_2, rel_zh = order // 32, (order // 8) % 4, (order // 2) % 4, order % 2

    def slots_of(x_rel, y_rel):
        return index_of(my_zh ^ rel_zh, (my_x + x_rel) % X, (my_y + y_rel) % Y, my_core ^ rel_core)

    summed = []
    for colour, (first, second) in enumerate((("x", "y"), ("y", "x"))):
        slots = slots_of(rel_1, rel_2) if first == "x" else slots_of(rel_2, rel_1)
        blocks = pick(owner_map, slots)
        partial = lax.dot_general(
            hidden_acts,
            masked[:, colour * half : (colour + 1) * half],
            (((0,), (0,)), ((), ())),
            preferred_element_type=f32,
        ).astype(bf16)
        slotted = pick(partial.reshape(workers, block, half), blocks)
        slotted = slotted.reshape(CORE, 4, 4, ZH, block, half)
        arrived = to_core(slotted[1])
        pair = [
            (slotted[0, d].astype(f32) + arrived[d].astype(f32)).astype(bf16) for d in range(4)
        ]
        got = [shift(pair[d], first, d) for d in (2, 1, 3)]
        line = [
            sum((g[e].astype(f32) for g in got), pair[0][e].astype(f32)) for e in range(4)
        ]
        got = [shift(line[d].astype(bf16), second, d) for d in (2, 1, 3)]
        summed.append(
            sum((g.astype(f32) for g in got), line[0].astype(bf16).astype(f32))
        )
    ready = jnp.concatenate(summed, axis=-1)
    summed = ready[0] + to_zh(ready[1])

    largest = jnp.max(jnp.abs(masked)).astype(f32) * jnp.max(jnp.abs(down_weight)).astype(f32)
    unit = jnp.maximum(largest * (columns / 32768.0), 1e-30)
    scale = 1.0 / unit
    ways = lax.axis_size("mp")

    def share_of(offset):
        part = lax.dynamic_slice_in_dim(
            down_weight, ((my_mp + offset) % ways) * shares, shares, 0
        )
        return lax.dot_general(
            masked, part, (((1,), (1,)), ((), ())), preferred_element_type=f32
        )

    result = None
    for offset in (2, 1, 3):
        ring = [(source, (source + offset) % ways) for source in range(ways)]
        sent = (share_of(offset) * scale).astype(f16)
        other = lax.ppermute(sent, "mp", ring).astype(f32) * lax.ppermute(unit, "mp", ring)
        result = other if result is None else result + other
    input_grads = (result + share_of(0)).astype(bf16)

    grad = summed / total
    moment1_new = beta_one * moment1 + (1.0 - beta_one) * grad
    second = beta_two * moment2.astype(f32) + (1.0 - beta_two) * grad * grad
    moment2_new = second.astype(bf16)
    master_new = master - learn_rate * (moment1_new / correct_one) / (
        jnp.sqrt(second / correct_two) + epsilon
    )

    weights = master_new.astype(bf16)
    both = jnp.stack([weights, to_zh(weights)])
    order = jnp.arange(workers // 2, dtype=jnp.int32)
    rel_2, rel_1, rel_zh = order // 8, (order // 2) % 4, order % 2
    halves = []
    for colour, (first, second) in enumerate((("x", "y"), ("y", "x"))):
        part = both[:, :, colour * half : (colour + 1) * half]
        line = jnp.concatenate([part] + [shift(part, first, d) for d in (1, 2, 3)])
        pieces = [line] + [shift(line, second, d) for d in (1, 2, 3)]
        pieces += [to_core(piece) for piece in pieces]
        x_rel, y_rel = (rel_1, rel_2) if first == "x" else (rel_2, rel_1)
        slots = jnp.concatenate(
            [
                index_of(my_zh ^ rel_zh, (my_x - x_rel) % X, (my_y - y_rel) % Y, my_core ^ other)
                for other in range(2)
            ]
        )
        halves.append((pieces, pick(owner_map, slots)))
    weights_new = place_blocks(halves, workers, block, half).reshape(hidden, columns)
    return (master_new, moment1_new, moment2_new, weights_new, input_grads)


def solution(mesh):
    in_specs = (
        P("dp", None),
        P("dp", "mp"),
        P("dp"),
        P(None, "mp"),
        P(),
        P("dp", "mp"),
        P("dp", "mp"),
        P("dp", "mp"),
    )
    out_specs = (P("dp", "mp"), P("dp", "mp"), P("dp", "mp"), P(None, "mp"), P("dp", "mp"))
    return jax.shard_map(
        per_device, mesh=mesh, in_specs=in_specs, out_specs=out_specs, check_vma=False
    )
```

```python
import jax
import jax.numpy as jnp
from jax import lax
from jax.experimental import pallas as pl
from jax.experimental.pallas import tpu as pltpu
from jax.sharding import PartitionSpec as P

beta_one = 0.9
beta_two = 0.95
learn_rate = 0.0003
epsilon = 1e-08
correct_one = 1.0 - 0.9**50
correct_two = 1.0 - 0.95**50


ZH, X, Y, CORE = 2, 4, 4, 2
f32, bf16, i16 = jnp.float32, jnp.bfloat16, jnp.int16
DIGITS = 6
EXTRA = 128
GROUP = 32


def index_of(zh, x, y, core):
    return ((zh * X + x) * Y + y) * CORE + core


def move(value, to):
    pairs = [
        (index_of(z, x, y, c), index_of(*to(z, x, y, c)))
        for z in range(ZH)
        for x in range(X)
        for y in range(Y)
        for c in range(CORE)
    ]
    return lax.ppermute(value, "dp", pairs)


def to_core(value):
    return move(value, lambda z, x, y, c: (z, x, y, 1 - c))


def to_zh(value):
    return move(value, lambda z, x, y, c: (1 - z, x, y, c))


def shift(value, ring, by):
    if ring == "x":
        return move(value, lambda z, x, y, c: (z, (x + by) % X, y, c))
    return move(value, lambda z, x, y, c: (z, x, (y + by) % Y, c))


def pick(array, index):
    return array.at[index].get(mode="promise_in_bounds")


def weight_partials(acts, grads, count, place, interpret=False):
    tokens, hidden = acts.shape
    columns = grads.shape[1]
    blocks = place.shape[0]
    height = hidden // blocks
    wide = 256
    steps = columns // wide
    near = blocks // 2

    def kernel(count_ref, place_ref, acts_ref, grads_ref, keep_ref, send_ref, turned, ordered):
        step = pl.program_id(0)

        @pl.when(step == 0)
        def _():
            chunk = 256
            for at in range(0, tokens, chunk):
                live = lax.broadcasted_iota(jnp.int32, (chunk, hidden), 0) + at < count_ref[0]
                part = jnp.where(live, acts_ref[pl.ds(at, chunk), :].astype(f32), 0.0)
                turned[:, pl.ds(at, chunk)] = part.T.astype(bf16)

        @pl.when(step < steps)
        def _():
            part = jnp.dot(turned[...], grads_ref[...], preferred_element_type=f32).astype(bf16)
            for b in range(blocks):
                ordered[place_ref[b]] = part[b * height : (b + 1) * height]
            keep_ref[...] = ordered[:near]
            send_ref[...] = ordered[near:]

        @pl.when(step == steps)
        def _():
            lane = lax.broadcasted_iota(jnp.int32, (near, height, wide), 2)
            digit = (count_ref[0] >> jnp.minimum(2 * lane, 30)) & 3
            value = digit.astype(f32).astype(bf16)
            keep_ref[...] = value
            send_ref[...] = value

    out = jax.ShapeDtypeStruct((near, height, columns + EXTRA), bf16)
    spec = pl.BlockSpec((near, height, wide), lambda n: (0, 0, n))
    return pl.pallas_call(
        kernel,
        grid=(steps + 1,),
        out_shape=(out, out),
        in_specs=[
            pl.BlockSpec(memory_space=pltpu.SMEM),
            pl.BlockSpec(memory_space=pltpu.SMEM),
            pl.BlockSpec((tokens, hidden), lambda n: (0, 0)),
            pl.BlockSpec((tokens, wide), lambda n: (0, jnp.minimum(n, steps - 1))),
        ],
        out_specs=(spec, spec),
        scratch_shapes=[pltpu.VMEM((hidden, tokens), bf16), pltpu.VMEM((blocks, height, wide), bf16)],
        interpret=interpret,
    )(count, place, acts, grads)


def input_shares(grads, weight, count, mine, ways, interpret=False):
    tokens, columns = grads.shape
    hidden = weight.shape[0]
    width = hidden // ways
    tall = 512
    groups = tall // GROUP
    extra = 16

    def kernel(count_ref, mine_ref, grads_ref, weight_ref, own_ref, *coded):
        step = pl.program_id(0)
        live = lax.broadcasted_iota(jnp.int32, (tall, width), 0) + step * tall < count_ref[0]
        for offset in (*range(1, ways), 0):
            at = lax.rem(mine_ref[0] + offset, ways) * width
            part = weight_ref[pl.ds(pl.multiple_of(at, width), width), :]
            share = lax.dot_general(
                grads_ref[...], part, (((1,), (1,)), ((), ())), preferred_element_type=f32
            )
            share = jnp.where(live, share, 0.0)
            if offset == 0:
                own_ref[...] = share
                continue
            out = coded[offset - 1]
            largest = jnp.max(jnp.abs(share).reshape(groups, GROUP, width), axis=1)
            largest = jnp.max(largest, axis=1, keepdims=True)
            power = jnp.floor(jnp.log2(32000.0 / jnp.maximum(largest, 1e-25)))
            power = jnp.broadcast_to(jnp.minimum(power, 90.0), (groups, width))
            factor = jnp.exp2(power)
            for g in range(groups):
                code = jnp.round(share[g * GROUP : (g + 1) * GROUP] * factor[g : g + 1])
                out[0, g * GROUP : (g + 1) * GROUP, :] = code.astype(jnp.int32).astype(i16)
            out[0, tall : tall + extra, :] = power.astype(jnp.int32).astype(i16)

    code = jax.ShapeDtypeStruct((tokens // tall, tall + extra, width), i16)
    return pl.pallas_call(
        kernel,
        grid=(tokens // tall,),
        out_shape=(jax.ShapeDtypeStruct((tokens, width), f32),) + (code,) * (ways - 1),
        in_specs=[
            pl.BlockSpec(memory_space=pltpu.SMEM),
            pl.BlockSpec(memory_space=pltpu.SMEM),
            pl.BlockSpec((tall, columns), lambda n: (n, 0)),
            pl.BlockSpec((hidden, columns), lambda n: (0, 0)),
        ],
        out_specs=(pl.BlockSpec((tall, width), lambda n: (n, 0)),)
        + (pl.BlockSpec((1, tall + extra, width), lambda n: (n, 0, 0)),) * (ways - 1),
        interpret=interpret,
    )(count, mine, grads, weight)


def add_shares(own, coded, interpret=False):
    tokens, width = own.shape
    steps, padded, _ = coded[0].shape
    tall = tokens // steps
    groups = tall // GROUP

    def kernel(own_ref, *refs):
        out = refs[-1]
        factors = [
            jnp.exp2(-ref[0, tall:padded, :].astype(jnp.int32).astype(f32)) for ref in refs[:-1]
        ]
        for g in range(groups):
            rows = slice(g * GROUP, (g + 1) * GROUP)
            value = own_ref[rows]
            for ref, factor in zip(refs[:-1], factors):
                value += ref[0, rows, :].astype(jnp.int32).astype(f32) * factor[g : g + 1]
            out[rows] = value.astype(bf16)

    return pl.pallas_call(
        kernel,
        grid=(steps,),
        out_shape=jax.ShapeDtypeStruct((tokens, width), bf16),
        in_specs=[pl.BlockSpec((tall, width), lambda n: (n, 0))]
        + [pl.BlockSpec((1, padded, width), lambda n: (n, 0, 0))] * len(coded),
        out_specs=pl.BlockSpec((tall, width), lambda n: (n, 0)),
        interpret=interpret,
    )(own, *coded)


def place_blocks(pieces, rows_of, interpret=False):
    counts = [piece.shape[0] for piece in pieces]
    shape = (sum(counts), *pieces[0].shape[1:])

    def kernel(rows_ref, *refs):
        sources, out, held, got, sent = refs[: len(pieces)], *refs[len(pieces) :]
        starts = [sum(counts[:i]) for i in range(len(pieces))]
        reads = [
            pltpu.make_async_copy(source, held.at[pl.ds(start, count)], got.at[i])
            for i, (source, start, count) in enumerate(zip(sources, starts, counts))
        ]
        for read in reads:
            read.start()
        for read, start, count in zip(reads, starts, counts):
            read.wait()
            for b in range(start, start + count):
                pltpu.make_async_copy(held.at[b], out.at[rows_ref[b]], sent).start()
        pltpu.make_async_copy(held, out, sent).wait()

    return pl.pallas_call(
        kernel,
        out_shape=jax.ShapeDtypeStruct(shape, bf16),
        in_specs=[pl.BlockSpec(memory_space=pltpu.SMEM)]
        + [pl.BlockSpec(memory_space=pl.ANY)] * len(pieces),
        out_specs=pl.BlockSpec(memory_space=pl.ANY),
        scratch_shapes=[
            pltpu.VMEM(shape, bf16),
            pltpu.SemaphoreType.DMA((len(pieces),)),
            pltpu.SemaphoreType.DMA,
        ],
        interpret=interpret,
    )(rows_of, *pieces)


def per_device(
    hidden_acts, out_grads, token_counts, down_weight, owner_map, master, moment1, moment2
):
    columns = out_grads.shape[1]
    hidden = hidden_acts.shape[1]
    workers = owner_map.shape[0]
    block = hidden // workers
    me = lax.axis_index("dp")
    my_core, my_y, my_x, my_zh = me % 2, (me // 2) % 4, (me // 8) % 4, me // 32
    my_mp = lax.axis_index("mp").astype(jnp.int32).reshape(1)
    ways = lax.axis_size("mp")

    slot = jnp.zeros((workers,), jnp.int32).at[owner_map].set(lax.iota(jnp.int32, workers))
    rel_core, rel_zh = (slot % 2) ^ my_core, (slot // 32) ^ my_zh
    far_x, far_y = ((slot // 8) % 4 - my_x) % 4, ((slot // 2) % 4 - my_y) % 4
    near = jnp.where(rel_zh == 0, far_x * 4 + far_y, far_y * 4 + far_x)
    place = rel_core * 32 + rel_zh * 16 + near

    keep, send = weight_partials(hidden_acts, out_grads, token_counts, place)
    arrived = to_core(send)
    out_grads, keep = lax.optimization_barrier((out_grads, keep))
    own, *coded = input_shares(out_grads, down_weight, token_counts, my_mp, ways)

    pair = [
        (keep[4 * i : 4 * i + 4].astype(f32) + arrived[4 * i : 4 * i + 4].astype(f32)).astype(bf16)
        for i in range(8)
    ]
    rings = (("x", "y"), ("y", "x"))
    lines = []
    for colour, (first, _) in enumerate(rings):
        mine, *away = pair[4 * colour : 4 * colour + 4]
        got = [shift(away[d - 1], first, d) for d in (2, 1, 3)]
        lines.append(
            [
                sum((g[e].astype(f32) for g in got), mine[e].astype(f32)).astype(bf16)
                for e in range(4)
            ]
        )
    sums = []
    for (_, second), line in zip(rings, lines):
        got = [shift(line[d], second, d) for d in (2, 1, 3)]
        sums.append(sum((g.astype(f32) for g in got), line[0].astype(f32)))
    summed = sums[0] + to_zh(sums[1])

    arrived = []
    for offset in range(1, ways):
        ring = [(source, (source + offset) % ways) for source in range(ways)]
        arrived.append(lax.ppermute(coded[offset - 1], "mp", ring))
    input_grads = add_shares(own, arrived)

    digits = summed[0, columns : columns + DIGITS]
    total = jnp.sum(digits * (4.0 ** jnp.arange(DIGITS, dtype=f32)))
    grad = summed[:, :columns] / total
    moment1_new = beta_one * moment1 + (1.0 - beta_one) * grad
    second = beta_two * moment2.astype(f32) + (1.0 - beta_two) * grad * grad
    moment2_new = second.astype(bf16)
    master_new = master - learn_rate * (moment1_new / correct_one) / (
        jnp.sqrt(second / correct_two) + epsilon
    )

    weights = master_new.astype(bf16)[None]
    pieces = []
    for part, (first, second) in zip((weights, to_zh(weights)), rings):
        line = jnp.concatenate([part] + [shift(part, first, d) for d in (1, 2, 3)])
        pieces += [line] + [shift(line, second, d) for d in (1, 2, 3)]
    pieces += [to_core(piece) for piece in pieces]
    order = jnp.arange(workers, dtype=jnp.int32)
    rel_core, rel_zh, rel_2, rel_1 = order // 32, (order // 16) % 2, (order // 4) % 4, order % 4
    x_rel, y_rel = jnp.where(rel_zh == 0, rel_1, rel_2), jnp.where(rel_zh == 0, rel_2, rel_1)
    slots = index_of(my_zh ^ rel_zh, (my_x - x_rel) % 4, (my_y - y_rel) % 4, my_core ^ rel_core)
    weights_new = place_blocks(pieces, pick(owner_map, slots)).reshape(hidden, columns)
    return (master_new, moment1_new, moment2_new, weights_new, input_grads)


def solution(mesh):
    in_specs = (
        P("dp", None),
        P("dp", "mp"),
        P("dp"),
        P(None, "mp"),
        P(),
        P("dp", "mp"),
        P("dp", "mp"),
        P("dp", "mp"),
    )
    out_specs = (P("dp", "mp"), P("dp", "mp"), P("dp", "mp"), P(None, "mp"), P("dp", "mp"))
    return jax.shard_map(
        per_device, mesh=mesh, in_specs=in_specs, out_specs=out_specs, check_vma=False
    )
```

```python
import jax
import jax.numpy as jnp
from jax import lax
from jax.experimental import pallas as pl
from jax.experimental.pallas import tpu as pltpu
from jax.sharding import PartitionSpec as P


beta_one = 0.9
beta_two = 0.95
learn_rate = 0.0003
epsilon = 1e-08
correct_one = 1.0 - 0.9**50
correct_two = 1.0 - 0.95**50


ZH, X, Y, CORE = 2, 4, 4, 2
f32, bf16, i16 = jnp.float32, jnp.bfloat16, jnp.int16
DIGITS = 6
EXTRA = 128
GROUP = 32


def index_of(zh, x, y, core):
    return ((zh * X + x) * Y + y) * CORE + core


def move(value, to):
    pairs = [
        (index_of(z, x, y, c), index_of(*to(z, x, y, c)))
        for z in range(ZH)
        for x in range(X)
        for y in range(Y)
        for c in range(CORE)
    ]
    return lax.ppermute(value, "dp", pairs)


def to_core(value):
    return move(value, lambda z, x, y, c: (z, x, y, 1 - c))


def to_zh(value):
    return move(value, lambda z, x, y, c: (1 - z, x, y, c))


def shift(value, ring, by):
    if ring == "x":
        return move(value, lambda z, x, y, c: (z, (x + by) % X, y, c))
    return move(value, lambda z, x, y, c: (z, x, (y + by) % Y, c))


def relative_slot(position, me):
    core, zh, first, second = position // 32, (position // 16) % 2, (position // 4) % 4, position % 4
    far_x, far_y = (second, first) if zh else (first, second)
    x = lax.rem(lax.div(me, 8) + far_x, 4)
    y = lax.rem(lax.div(me, 2) + far_y, 4)
    my_zh, my_core = lax.div(me, 32), lax.rem(me, 2)
    return index_of(1 - my_zh if zh else my_zh, x, y, 1 - my_core if core else my_core)


def weight_partials(acts, grads, count, owner_map, me, interpret=False):
    tokens, hidden = acts.shape
    columns = grads.shape[1]
    blocks = owner_map.shape[0]
    height = hidden // blocks
    wide = 512
    steps = columns // wide
    near = blocks // 2
    chunk = 512
    parts = tokens // chunk

    def kernel(count_ref, map_ref, me_ref, acts_ref, grads_ref, keep_ref, send_ref, raw, turned, part, sems):
        step = pl.program_id(0)

        def put():
            for p in range(blocks):
                start = pl.multiple_of(map_ref[relative_slot(p, me_ref[0])] * height, height)
                out = keep_ref if p < near else send_ref
                out[p % near] = part[pl.ds(start, height), :].astype(bf16)

        @pl.when(step == 0)
        def _():
            loads = [
                pltpu.make_async_copy(
                    acts_ref.at[pl.ds(i * chunk, chunk)], raw.at[pl.ds(i * chunk, chunk)], sems.at[i]
                )
                for i in range(parts)
            ]
            for load in loads:
                load.start()
            for i, load in enumerate(loads):
                rows = pl.ds(i * chunk, chunk)
                load.wait()
                live = lax.broadcasted_iota(jnp.int32, (1, chunk), 1) + i * chunk < count_ref[0]
                flipped = raw[rows, :].T * jnp.where(live, 1.0, 0.0).astype(bf16)
                turned[:, rows] = flipped
                value = jnp.dot(flipped, grads_ref[rows, :], preferred_element_type=f32)
                if i == 0:
                    part[...] = value
                else:
                    part[...] += value
            put()

        @pl.when((step > 0) & (step < steps))
        def _():
            part[...] = jnp.dot(turned[...], grads_ref[...], preferred_element_type=f32)
            put()

        @pl.when(step == steps)
        def _():
            lane = lax.broadcasted_iota(jnp.int32, (near, height, EXTRA), 2)
            digit = (count_ref[0] >> jnp.minimum(2 * lane, 30)) & 3
            value = digit.astype(f32).astype(bf16)
            keep_ref[:, :, :EXTRA] = value
            send_ref[:, :, :EXTRA] = value

    out = jax.ShapeDtypeStruct((near, height, columns + EXTRA), bf16)
    spec = pl.BlockSpec((near, height, wide), lambda n: (0, 0, n))
    return pl.pallas_call(
        kernel,
        grid=(steps + 1,),
        out_shape=(out, out),
        in_specs=[pl.BlockSpec(memory_space=pltpu.SMEM)] * 3
        + [
            pl.BlockSpec(memory_space=pl.ANY),
            pl.BlockSpec((tokens, wide), lambda n: (0, jnp.minimum(n, steps - 1))),
        ],
        out_specs=(spec, spec),
        scratch_shapes=[
            pltpu.VMEM((tokens, hidden), bf16),
            pltpu.VMEM((hidden, tokens), bf16),
            pltpu.VMEM((hidden, wide), f32),
            pltpu.SemaphoreType.DMA((parts,)),
        ],
        compiler_params=pltpu.CompilerParams(vmem_limit_bytes=60 * 2**20),
        interpret=interpret,
    )(count, owner_map, me, acts, grads)


def input_shares(grads, weight, count, mine, ways, interpret=False):
    tokens, columns = grads.shape
    hidden = weight.shape[0]
    width = hidden // ways
    tall = 256
    groups = tall // GROUP
    extra = 16

    def kernel(count_ref, mine_ref, grads_ref, weight_ref, own_ref, *refs):
        coded, held, sems = refs[:-2], refs[-2], refs[-1]
        step = pl.program_id(0)
        live = lax.broadcasted_iota(jnp.int32, (tall, width), 0) + step * tall < count_ref[0]
        order = (*range(1, ways), 0)

        def load(offset):
            at = lax.rem(mine_ref[0] + offset, ways) * width
            return pltpu.make_async_copy(
                weight_ref.at[pl.ds(pl.multiple_of(at, width), width)], held.at[offset], sems.at[offset]
            )

        @pl.when(step == 0)
        def _():
            for offset in order:
                load(offset).start()

        for offset in order:

            @pl.when(step == 0)
            def _(offset=offset):
                load(offset).wait()

            share = lax.dot_general(
                grads_ref[...], held[offset], (((1,), (1,)), ((), ())), preferred_element_type=f32
            )
            share = jnp.where(live, share, 0.0)
            if offset == 0:
                own_ref[...] = share
                continue
            out = coded[offset - 1]
            largest = jnp.max(jnp.abs(share).reshape(groups, GROUP, width), axis=1)
            largest = jnp.max(largest, axis=1, keepdims=True)
            power = jnp.floor(jnp.log2(32000.0 / jnp.maximum(largest, 1e-25)))
            power = jnp.broadcast_to(jnp.minimum(power, 90.0), (groups, width))
            factor = jnp.exp2(power)
            for g in range(groups):
                code = jnp.round(share[g * GROUP : (g + 1) * GROUP] * factor[g : g + 1])
                out[0, g * GROUP : (g + 1) * GROUP, :] = code.astype(jnp.int32).astype(i16)
            power = jnp.concatenate([power] * (extra // groups), axis=0)
            out[0, tall : tall + extra, :] = power.astype(jnp.int32).astype(i16)

    code = jax.ShapeDtypeStruct((tokens // tall, tall + extra, width), i16)
    return pl.pallas_call(
        kernel,
        grid=(tokens // tall,),
        out_shape=(jax.ShapeDtypeStruct((tokens, width), f32),) + (code,) * (ways - 1),
        in_specs=[pl.BlockSpec(memory_space=pltpu.SMEM)] * 2
        + [
            pl.BlockSpec((tall, columns), lambda n: (n, 0)),
            pl.BlockSpec(memory_space=pl.ANY),
        ],
        out_specs=(pl.BlockSpec((tall, width), lambda n: (n, 0)),)
        + (pl.BlockSpec((1, tall + extra, width), lambda n: (n, 0, 0)),) * (ways - 1),
        scratch_shapes=[pltpu.VMEM((ways, width, columns), bf16), pltpu.SemaphoreType.DMA((ways,))],
        compiler_params=pltpu.CompilerParams(vmem_limit_bytes=60 * 2**20),
        interpret=interpret,
    )(count, mine, grads, weight)


def add_shares(own, coded, interpret=False):
    tokens, width = own.shape
    steps, padded, _ = coded[0].shape
    tall = tokens // steps
    groups = tall // GROUP

    def kernel(own_ref, *refs):
        out = refs[-1]

        def add(step, carry):
            base = pl.multiple_of(step * tall, tall)
            factors = [
                jnp.exp2(-ref[step, tall:padded, :].astype(jnp.int32).astype(f32))
                for ref in refs[:-1]
            ]
            for g in range(groups):
                rows = pl.ds(base + g * GROUP, GROUP)
                value = own_ref[rows, :]
                for ref, factor in zip(refs[:-1], factors):
                    code = ref[step, g * GROUP : (g + 1) * GROUP, :]
                    value += code.astype(jnp.int32).astype(f32) * factor[g : g + 1]
                out[rows, :] = value.astype(bf16)
            return carry

        lax.fori_loop(0, steps, add, 0)

    whole = pl.BlockSpec(memory_space=pltpu.VMEM)
    return pl.pallas_call(
        kernel,
        out_shape=jax.ShapeDtypeStruct((tokens, width), bf16),
        in_specs=[whole] * (1 + len(coded)),
        out_specs=whole,
        compiler_params=pltpu.CompilerParams(vmem_limit_bytes=12 * 2**20),
        interpret=interpret,
    )(own, *coded)


def place_blocks(pieces, owner_map, me, interpret=False):
    counts = [piece.shape[0] for piece in pieces]
    shape = (sum(counts), *pieces[0].shape[1:])

    def source_slot(position, me):
        core, zh, second, first = position // 32, (position // 16) % 2, (position // 4) % 4, position % 4
        far_x, far_y = (second, first) if zh else (first, second)
        x = lax.rem(lax.div(me, 8) + 4 - far_x, 4)
        y = lax.rem(lax.div(me, 2) + 4 - far_y, 4)
        my_zh, my_core = lax.div(me, 32), lax.rem(me, 2)
        return index_of(1 - my_zh if zh else my_zh, x, y, 1 - my_core if core else my_core)

    def kernel(map_ref, me_ref, *refs):
        sources, out, sent = refs[: len(pieces)], *refs[len(pieces) :]
        at = 0
        for source, count in zip(sources, counts):
            for b in range(count):
                row = map_ref[source_slot(at + b, me_ref[0])]
                pltpu.make_async_copy(source.at[b], out.at[row], sent).start()
            at += count
        pltpu.make_async_copy(out, out, sent).wait()

    return pl.pallas_call(
        kernel,
        out_shape=jax.ShapeDtypeStruct(shape, bf16),
        in_specs=[pl.BlockSpec(memory_space=pltpu.SMEM)] * 2
        + [pl.BlockSpec(memory_space=pltpu.VMEM)] * len(pieces),
        out_specs=pl.BlockSpec(memory_space=pl.ANY),
        scratch_shapes=[pltpu.SemaphoreType.DMA],
        compiler_params=pltpu.CompilerParams(vmem_limit_bytes=12 * 2**20),
        interpret=interpret,
    )(owner_map, me, *pieces)


def per_device(
    hidden_acts, out_grads, token_counts, down_weight, owner_map, master, moment1, moment2
):
    columns = out_grads.shape[1]
    hidden = hidden_acts.shape[1]
    me = lax.axis_index("dp").astype(jnp.int32).reshape(1)
    my_mp = lax.axis_index("mp").astype(jnp.int32).reshape(1)
    ways = lax.axis_size("mp")
    rings = (("x", "y"), ("y", "x"))

    def pass_share(coded, offset):
        ring = [(source, (source + offset) % ways) for source in range(ways)]
        return lax.ppermute(coded[offset - 1], "mp", ring)

    keep, send = weight_partials(hidden_acts, out_grads, token_counts, owner_map, me)
    arrived = to_core(send)
    out_grads, keep = lax.optimization_barrier((out_grads, keep))
    own, *coded = input_shares(out_grads, down_weight, token_counts, my_mp, ways)
    arrived, own = lax.optimization_barrier((arrived, own))
    shares = [pass_share(coded, 1), pass_share(coded, 3)]

    pair = [
        (keep[4 * i : 4 * i + 4].astype(f32) + arrived[4 * i : 4 * i + 4].astype(f32)).astype(bf16)
        for i in range(8)
    ]
    got = [
        [shift(pair[4 * colour + d], first, d) for d in (2, 1, 3)]
        for colour, (first, _) in enumerate(rings)
    ]
    got = lax.optimization_barrier(got)
    lines = [
        [
            sum((g[e].astype(f32) for g in got[colour]), pair[4 * colour][e].astype(f32)).astype(bf16)
            for e in range(4)
        ]
        for colour in range(2)
    ]
    got = [
        [shift(line[d], second, d) for d in (2, 1, 3)] for line, (_, second) in zip(lines, rings)
    ]
    got = lax.optimization_barrier(got)
    sums = [
        sum((g.astype(f32) for g in group), line[0].astype(f32)) for group, line in zip(got, lines)
    ]
    summed = sums[0] + to_zh(sums[1])

    digits = summed[0, columns : columns + DIGITS]
    total = jnp.sum(digits * (4.0 ** jnp.arange(DIGITS, dtype=f32)))
    grad = summed[:, :columns] / total
    moment1_new = beta_one * moment1 + (1.0 - beta_one) * grad
    second = beta_two * moment2.astype(f32) + (1.0 - beta_two) * grad * grad
    moment2_new = second.astype(bf16)
    master_new = master - learn_rate * (moment1_new / correct_one) / (
        jnp.sqrt(second / correct_two) + epsilon
    )

    weights = master_new.astype(bf16)[None]
    other = to_zh(weights)
    shares.append(pass_share(coded, 2))
    pieces = []
    for part, (first, second) in zip((weights, other), rings):
        line = jnp.concatenate([part] + [shift(part, first, d) for d in (1, 2, 3)])
        pieces += [line] + [shift(line, second, d) for d in (1, 2, 3)]
    pieces += [to_core(piece) for piece in pieces]
    input_grads = add_shares(own, shares)
    weights_new = place_blocks(pieces, owner_map, me).reshape(hidden, columns)
    return (master_new, moment1_new, moment2_new, weights_new, input_grads)


def solution(mesh):
    in_specs = (
        P("dp", None),
        P("dp", "mp"),
        P("dp"),
        P(None, "mp"),
        P(),
        P("dp", "mp"),
        P("dp", "mp"),
        P("dp", "mp"),
    )
    out_specs = (P("dp", "mp"), P("dp", "mp"), P("dp", "mp"), P(None, "mp"), P("dp", "mp"))
    return jax.shard_map(per_device, mesh=mesh, in_specs=in_specs, out_specs=out_specs, check_vma=False)
```

```python
import jax
import jax.numpy as jnp
from jax import lax
from jax.experimental import pallas as pl
from jax.experimental.pallas import tpu as pltpu
from jax.sharding import PartitionSpec as P


beta_one = 0.9
beta_two = 0.95
learn_rate = 0.0003
epsilon = 1e-08
correct_one = 1.0 - 0.9**50
correct_two = 1.0 - 0.95**50


ZH, X, Y, CORE = 2, 4, 4, 2
f32, bf16, i16 = jnp.float32, jnp.bfloat16, jnp.int16
DIGITS = 6
EXTRA = 128
GROUP = 32


def index_of(zh, x, y, core):
    return ((zh * X + x) * Y + y) * CORE + core


def move(value, to):
    pairs = [
        (index_of(z, x, y, c), index_of(*to(z, x, y, c)))
        for z in range(ZH)
        for x in range(X)
        for y in range(Y)
        for c in range(CORE)
    ]
    return lax.ppermute(value, "dp", pairs)


def to_core(value):
    return move(value, lambda z, x, y, c: (z, x, y, 1 - c))


def to_zh(value):
    return move(value, lambda z, x, y, c: (1 - z, x, y, c))


def shift(value, ring, by):
    if ring == "x":
        return move(value, lambda z, x, y, c: (z, (x + by) % X, y, c))
    return move(value, lambda z, x, y, c: (z, x, (y + by) % Y, c))


def relative_slot(position, me):
    core, zh, first, second = position // 32, (position // 16) % 2, (position // 4) % 4, position % 4
    far_x, far_y = (second, first) if zh else (first, second)
    x = lax.rem(lax.div(me, 8) + far_x, 4)
    y = lax.rem(lax.div(me, 2) + far_y, 4)
    my_zh, my_core = lax.div(me, 32), lax.rem(me, 2)
    return index_of(1 - my_zh if zh else my_zh, x, y, 1 - my_core if core else my_core)


def weight_partials(acts, grads, count, owner_map, me, interpret=False):
    tokens, hidden = acts.shape
    columns = grads.shape[1]
    blocks = owner_map.shape[0]
    height = hidden // blocks
    wide = 512
    steps = columns // wide
    near = blocks // 2
    chunk = 512
    parts = tokens // chunk

    def kernel(count_ref, map_ref, me_ref, acts_ref, grads_ref, keep_ref, send_ref, raw, turned, part, sems):
        step = pl.program_id(0)

        def put():
            for p in range(blocks):
                start = pl.multiple_of(map_ref[relative_slot(p, me_ref[0])] * height, height)
                out = keep_ref if p < near else send_ref
                out[p % near] = part[pl.ds(start, height), :].astype(bf16)

        @pl.when(step == 0)
        def _():
            loads = [
                pltpu.make_async_copy(
                    acts_ref.at[pl.ds(i * chunk, chunk)], raw.at[pl.ds(i * chunk, chunk)], sems.at[i]
                )
                for i in range(parts)
            ]
            for load in loads:
                load.start()
            for i, load in enumerate(loads):
                rows = pl.ds(i * chunk, chunk)
                load.wait()
                live = lax.broadcasted_iota(jnp.int32, (1, chunk), 1) + i * chunk < count_ref[0]
                flipped = raw[rows, :].T * jnp.where(live, 1.0, 0.0).astype(bf16)
                turned[:, rows] = flipped
                value = jnp.dot(flipped, grads_ref[rows, :], preferred_element_type=f32)
                if i == 0:
                    part[...] = value
                else:
                    part[...] += value
            put()

        @pl.when((step > 0) & (step < steps))
        def _():
            part[...] = jnp.dot(turned[...], grads_ref[...], preferred_element_type=f32)
            put()

        @pl.when(step == steps)
        def _():
            lane = lax.broadcasted_iota(jnp.int32, (near, height, EXTRA), 2)
            digit = (count_ref[0] >> jnp.minimum(2 * lane, 30)) & 3
            value = digit.astype(f32).astype(bf16)
            keep_ref[:, :, :EXTRA] = value
            send_ref[:, :, :EXTRA] = value

    out = jax.ShapeDtypeStruct((near, height, columns + EXTRA), bf16)
    spec = pl.BlockSpec((near, height, wide), lambda n: (0, 0, n))
    return pl.pallas_call(
        kernel,
        grid=(steps + 1,),
        out_shape=(out, out),
        in_specs=[pl.BlockSpec(memory_space=pltpu.SMEM)] * 3
        + [
            pl.BlockSpec(memory_space=pl.ANY),
            pl.BlockSpec((tokens, wide), lambda n: (0, jnp.minimum(n, steps - 1))),
        ],
        out_specs=(spec, spec),
        scratch_shapes=[
            pltpu.VMEM((tokens, hidden), bf16),
            pltpu.VMEM((hidden, tokens), bf16),
            pltpu.VMEM((hidden, wide), f32),
            pltpu.SemaphoreType.DMA((parts,)),
        ],
        compiler_params=pltpu.CompilerParams(vmem_limit_bytes=60 * 2**20),
        interpret=interpret,
    )(count, owner_map, me, acts, grads)


def input_shares(grads, weight, count, mine, ways, offsets, interpret=False):
    tokens, columns = grads.shape
    hidden = weight.shape[0]
    width = hidden // ways
    tall = 512
    groups = tall // GROUP
    extra = 16

    def kernel(count_ref, mine_ref, grads_ref, *refs):
        step = pl.program_id(0)
        live = lax.broadcasted_iota(jnp.int32, (tall, width), 0) + step * tall < count_ref[0]
        for offset, part, out in zip(offsets, refs[: len(offsets)], refs[len(offsets) :]):
            share = lax.dot_general(
                grads_ref[...], part[...], (((1,), (1,)), ((), ())), preferred_element_type=f32
            )
            share = jnp.where(live, share, 0.0)
            if offset == 0:
                out[...] = share
                continue
            largest = jnp.max(jnp.abs(share).reshape(groups, GROUP, width), axis=1)
            largest = jnp.max(largest, axis=1, keepdims=True)
            power = jnp.floor(jnp.log2(32000.0 / jnp.maximum(largest, 1e-25)))
            power = jnp.broadcast_to(jnp.minimum(power, 90.0), (groups, width))
            factor = jnp.exp2(power)
            for g in range(groups):
                code = jnp.round(share[g * GROUP : (g + 1) * GROUP] * factor[g : g + 1])
                out[0, g * GROUP : (g + 1) * GROUP, :] = code.astype(jnp.int32).astype(i16)
            out[0, tall : tall + extra, :] = power.astype(jnp.int32).astype(i16)

    def part_of(offset):
        return pl.BlockSpec(
            (width, columns), lambda n, count, mine: (lax.rem(mine[0] + offset, ways), 0)
        )

    own = jax.ShapeDtypeStruct((tokens, width), f32)
    code = jax.ShapeDtypeStruct((tokens // tall, tall + extra, width), i16)
    own_spec = pl.BlockSpec((tall, width), lambda n, *_: (n, 0))
    code_spec = pl.BlockSpec((1, tall + extra, width), lambda n, *_: (n, 0, 0))
    return pl.pallas_call(
        kernel,
        grid_spec=pltpu.PrefetchScalarGridSpec(
            num_scalar_prefetch=2,
            grid=(tokens // tall,),
            in_specs=[pl.BlockSpec((tall, columns), lambda n, *_: (n, 0))]
            + [part_of(offset) for offset in offsets],
            out_specs=[own_spec if offset == 0 else code_spec for offset in offsets],
        ),
        out_shape=[own if offset == 0 else code for offset in offsets],
        compiler_params=pltpu.CompilerParams(vmem_limit_bytes=60 * 2**20),
        interpret=interpret,
    )(count, mine, grads, *[weight] * len(offsets))


def add_shares(own, coded, interpret=False):
    tokens, width = own.shape
    steps, padded, _ = coded[0].shape
    tall = tokens // steps
    groups = tall // GROUP

    def kernel(own_ref, *refs):
        out = refs[-1]

        def add(step, carry):
            base = pl.multiple_of(step * tall, tall)
            factors = [
                jnp.exp2(-ref[step, tall:padded, :].astype(jnp.int32).astype(f32))
                for ref in refs[:-1]
            ]
            for g in range(groups):
                rows = pl.ds(base + g * GROUP, GROUP)
                value = own_ref[rows, :]
                for ref, factor in zip(refs[:-1], factors):
                    code = ref[step, g * GROUP : (g + 1) * GROUP, :]
                    value += code.astype(jnp.int32).astype(f32) * factor[g : g + 1]
                out[rows, :] = value.astype(bf16)
            return carry

        lax.fori_loop(0, steps, add, 0)

    whole = pl.BlockSpec(memory_space=pltpu.VMEM)
    return pl.pallas_call(
        kernel,
        out_shape=jax.ShapeDtypeStruct((tokens, width), bf16),
        in_specs=[whole] * (1 + len(coded)),
        out_specs=whole,
        compiler_params=pltpu.CompilerParams(vmem_limit_bytes=12 * 2**20),
        interpret=interpret,
    )(own, *coded)


def place_blocks(pieces, owner_map, me, interpret=False):
    counts = [piece.shape[0] for piece in pieces]
    shape = (sum(counts), *pieces[0].shape[1:])

    def source_slot(position, me):
        core, zh, second, first = position // 32, (position // 16) % 2, (position // 4) % 4, position % 4
        far_x, far_y = (second, first) if zh else (first, second)
        x = lax.rem(lax.div(me, 8) + 4 - far_x, 4)
        y = lax.rem(lax.div(me, 2) + 4 - far_y, 4)
        my_zh, my_core = lax.div(me, 32), lax.rem(me, 2)
        return index_of(1 - my_zh if zh else my_zh, x, y, 1 - my_core if core else my_core)

    def kernel(map_ref, me_ref, *refs):
        sources, out, sent = refs[: len(pieces)], *refs[len(pieces) :]
        at = 0
        for source, count in zip(sources, counts):
            for b in range(count):
                row = map_ref[source_slot(at + b, me_ref[0])]
                pltpu.make_async_copy(source.at[b], out.at[row], sent).start()
            at += count
        pltpu.make_async_copy(out, out, sent).wait()

    return pl.pallas_call(
        kernel,
        out_shape=jax.ShapeDtypeStruct(shape, bf16),
        in_specs=[pl.BlockSpec(memory_space=pltpu.SMEM)] * 2
        + [pl.BlockSpec(memory_space=pltpu.VMEM)] * len(pieces),
        out_specs=pl.BlockSpec(memory_space=pl.ANY),
        scratch_shapes=[pltpu.SemaphoreType.DMA],
        compiler_params=pltpu.CompilerParams(vmem_limit_bytes=12 * 2**20),
        interpret=interpret,
    )(owner_map, me, *pieces)


def per_device(
    hidden_acts, out_grads, token_counts, down_weight, owner_map, master, moment1, moment2
):
    columns = out_grads.shape[1]
    hidden = hidden_acts.shape[1]
    me = lax.axis_index("dp").astype(jnp.int32).reshape(1)
    my_mp = lax.axis_index("mp").astype(jnp.int32).reshape(1)
    ways = lax.axis_size("mp")
    rings = (("x", "y"), ("y", "x"))

    def pass_share(coded, offset):
        ring = [(source, (source + offset) % ways) for source in range(ways)]
        return lax.ppermute(coded, "mp", ring)

    (up,) = input_shares(out_grads, down_weight, token_counts, my_mp, ways, (1,))
    shares = [pass_share(up, 1)]
    acts, _ = lax.optimization_barrier((hidden_acts, up))
    keep, send = weight_partials(acts, out_grads, token_counts, owner_map, me)
    arrived = to_core(send)
    states = jnp.stack([master, moment1, moment2.astype(f32)])
    other_states = to_zh(states)

    pair = [
        (keep[4 * i : 4 * i + 4].astype(f32) + arrived[4 * i : 4 * i + 4].astype(f32)).astype(bf16)
        for i in range(8)
    ]
    got = [
        [shift(pair[4 * colour + d], first, d) for d in (2, 1, 3)]
        for colour, (first, _) in enumerate(rings)
    ]
    got = lax.optimization_barrier(got)
    down, across, own = input_shares(
        out_grads, down_weight, token_counts, my_mp, ways, (3, 2, 0)
    )
    shares.append(pass_share(down, 3))
    lines = [
        [
            sum((g[e].astype(f32) for g in got[colour]), pair[4 * colour][e].astype(f32)).astype(bf16)
            for e in range(4)
        ]
        for colour in range(2)
    ]
    got = [
        [shift(line[d], second, d) for d in (2, 1, 3)]
        for line, (_, second) in zip(lines, rings)
    ]
    got = lax.optimization_barrier(got)
    sums = [
        sum((g.astype(f32) for g in group), line[0].astype(f32)) for group, line in zip(got, lines)
    ]
    sums = lax.optimization_barrier(jnp.stack(sums))
    theirs = to_zh(sums)
    shares.append(pass_share(across, 2))

    summed = sums + theirs[::-1]
    digits = summed[:, :1, columns : columns + DIGITS]
    total = jnp.sum(digits * (4.0 ** jnp.arange(DIGITS, dtype=f32)), axis=(1, 2), keepdims=True)
    grad = summed[:, :, :columns] / total
    old_master, old_first, old_second = jnp.stack([states, other_states], axis=1)
    moment1_new = beta_one * old_first + (1.0 - beta_one) * grad
    second = beta_two * old_second + (1.0 - beta_two) * grad * grad
    master_new = old_master - learn_rate * (moment1_new / correct_one) / (
        jnp.sqrt(second / correct_two) + epsilon
    )
    weights = master_new.astype(bf16)
    master_new, moment1_new, moment2_new = master_new[0], moment1_new[0], second[0].astype(bf16)

    got = [
        [shift(weights[colour : colour + 1], first, d) for d in (2, 1, 3)]
        for colour, (first, _) in enumerate(rings)
    ]
    got = lax.optimization_barrier(got)
    pieces = []
    for colour, (_, second) in enumerate(rings):
        two, one, three = got[colour]
        line = jnp.concatenate([weights[colour : colour + 1], one, two, three])
        two, one, three = [shift(line, second, d) for d in (2, 1, 3)]
        pieces += [line, one, two, three]
    pieces += [to_core(piece) for piece in pieces]
    input_grads = add_shares(own, shares)
    weights_new = place_blocks(pieces, owner_map, me).reshape(hidden, columns)
    return (master_new, moment1_new, moment2_new, weights_new, input_grads)


def solution(mesh):
    in_specs = (
        P("dp", None),
        P("dp", "mp"),
        P("dp"),
        P(None, "mp"),
        P(),
        P("dp", "mp"),
        P("dp", "mp"),
        P("dp", "mp"),
    )
    out_specs = (P("dp", "mp"), P("dp", "mp"), P("dp", "mp"), P(None, "mp"), P("dp", "mp"))
    return jax.shard_map(per_device, mesh=mesh, in_specs=in_specs, out_specs=out_specs, check_vma=False)
```

```python
import jax
import jax.numpy as jnp
from jax import lax
from jax.experimental import pallas as pl
from jax.experimental.pallas import tpu as pltpu
from jax.sharding import PartitionSpec as P


beta_one = 0.9
beta_two = 0.95
learn_rate = 0.0003
epsilon = 1e-08
correct_one = 1.0 - 0.9**50
correct_two = 1.0 - 0.95**50


ZH, X, Y, CORE = 2, 4, 4, 2
f32, bf16, i16 = jnp.float32, jnp.bfloat16, jnp.int16
DIGITS = 6
EXTRA = 128
GROUP = 32


def index_of(zh, x, y, core):
    return ((zh * X + x) * Y + y) * CORE + core


def move(value, to):
    pairs = [
        (index_of(z, x, y, c), index_of(*to(z, x, y, c)))
        for z in range(ZH)
        for x in range(X)
        for y in range(Y)
        for c in range(CORE)
    ]
    return lax.ppermute(value, "dp", pairs)


def to_core(value):
    return move(value, lambda z, x, y, c: (z, x, y, 1 - c))


def to_zh(value):
    return move(value, lambda z, x, y, c: (1 - z, x, y, c))


def shift(value, ring, by):
    if ring == "x":
        return move(value, lambda z, x, y, c: (z, (x + by) % X, y, c))
    return move(value, lambda z, x, y, c: (z, x, (y + by) % Y, c))


def relative_slot(position, me):
    core, zh, first, second = position // 32, (position // 16) % 2, (position // 4) % 4, position % 4
    far_x, far_y = (second, first) if zh else (first, second)
    x = lax.rem(lax.div(me, 8) + far_x, 4)
    y = lax.rem(lax.div(me, 2) + far_y, 4)
    my_zh, my_core = lax.div(me, 32), lax.rem(me, 2)
    return index_of(1 - my_zh if zh else my_zh, x, y, 1 - my_core if core else my_core)


def encode(share, out, at):
    tall, width = share.shape
    groups = tall // GROUP
    largest = jnp.max(jnp.abs(share).reshape(groups, GROUP, width), axis=1)
    largest = jnp.max(largest, axis=1, keepdims=True)
    power = jnp.floor(jnp.log2(32000.0 / jnp.maximum(largest, 1e-25)))
    power = jnp.broadcast_to(jnp.minimum(power, 90.0), (groups, width))
    factor = jnp.exp2(power)
    for g in range(groups):
        code = jnp.round(share[g * GROUP : (g + 1) * GROUP] * factor[g : g + 1])
        out[at, g * GROUP : (g + 1) * GROUP, :] = code.astype(jnp.int32).astype(i16)
    out[at, tall : tall + groups, :] = power.astype(jnp.int32).astype(i16)


TALL = 512


def weight_partials(acts, grads, weight, count, owner_map, me, mine, ways, interpret=False):
    tokens, hidden = acts.shape
    columns = grads.shape[1]
    blocks = owner_map.shape[0]
    height = hidden // blocks
    wide = 512
    steps = columns // wide
    near = blocks // 2
    chunk = 512
    parts = tokens // chunk

    width = hidden // ways
    extra = TALL // GROUP

    def kernel(
        count_ref, map_ref, me_ref, mine_ref, acts_ref, grads_ref, weight_ref,
        keep_ref, send_ref, up_ref, raw, turned, part, total, sems,
    ):
        step = pl.program_id(0)

        def add_up():
            value = lax.dot_general(
                grads_ref[...], weight_ref[...], (((1,), (1,)), ((), ())), preferred_element_type=f32
            )

            @pl.when(step == 0)
            def _():
                total[...] = value

            @pl.when(step > 0)
            def _():
                total[...] += value

        def put():
            for p in range(blocks):
                start = pl.multiple_of(map_ref[relative_slot(p, me_ref[0])] * height, height)
                out = keep_ref if p < near else send_ref
                out[p % near] = part[pl.ds(start, height), :].astype(bf16)

        @pl.when(step == 0)
        def _():
            loads = [
                pltpu.make_async_copy(
                    acts_ref.at[pl.ds(i * chunk, chunk)], raw.at[pl.ds(i * chunk, chunk)], sems.at[i]
                )
                for i in range(parts)
            ]
            for load in loads:
                load.start()
            for i, load in enumerate(loads):
                rows = pl.ds(i * chunk, chunk)
                load.wait()
                live = lax.broadcasted_iota(jnp.int32, (1, chunk), 1) + i * chunk < count_ref[0]
                flipped = raw[rows, :].T * jnp.where(live, 1.0, 0.0).astype(bf16)
                turned[:, rows] = flipped
                value = jnp.dot(flipped, grads_ref[rows, :], preferred_element_type=f32)
                if i == 0:
                    part[...] = value
                else:
                    part[...] += value
            put()
            add_up()

        @pl.when((step > 0) & (step < steps))
        def _():
            part[...] = jnp.dot(turned[...], grads_ref[...], preferred_element_type=f32)
            put()
            add_up()

        @pl.when(step == steps)
        def _():
            lane = lax.broadcasted_iota(jnp.int32, (near, height, EXTRA), 2)
            digit = (count_ref[0] >> jnp.minimum(2 * lane, 30)) & 3
            value = digit.astype(f32).astype(bf16)
            keep_ref[:, :, :EXTRA] = value
            send_ref[:, :, :EXTRA] = value
            for i in range(tokens // TALL):
                live = lax.broadcasted_iota(jnp.int32, (TALL, width), 0) + i * TALL < count_ref[0]
                encode(jnp.where(live, total[i * TALL : (i + 1) * TALL], 0.0), up_ref, i)

    out = jax.ShapeDtypeStruct((near, height, columns + EXTRA), bf16)
    spec = pl.BlockSpec((near, height, wide), lambda n, *_: (0, 0, n))
    code = (tokens // TALL, TALL + extra, width)
    return pl.pallas_call(
        kernel,
        grid_spec=pltpu.PrefetchScalarGridSpec(
            num_scalar_prefetch=4,
            grid=(steps + 1,),
            in_specs=[
                pl.BlockSpec(memory_space=pl.ANY),
                pl.BlockSpec((tokens, wide), lambda n, *_: (0, jnp.minimum(n, steps - 1))),
                pl.BlockSpec(
                    (width, wide),
                    lambda n, count, map, me, mine: (
                        lax.rem(mine[0] + 1, ways),
                        jnp.minimum(n, steps - 1),
                    ),
                ),
            ],
            out_specs=[spec, spec, pl.BlockSpec(code, lambda n, *_: (0, 0, 0))],
            scratch_shapes=[
                pltpu.VMEM((tokens, hidden), bf16),
                pltpu.VMEM((hidden, tokens), bf16),
                pltpu.VMEM((hidden, wide), f32),
                pltpu.VMEM((tokens, width), f32),
                pltpu.SemaphoreType.DMA((parts,)),
            ],
        ),
        out_shape=[out, out, jax.ShapeDtypeStruct(code, i16)],
        compiler_params=pltpu.CompilerParams(vmem_limit_bytes=60 * 2**20),
        interpret=interpret,
    )(count, owner_map, me, mine, acts, grads, weight)


def input_shares(grads, weight, count, mine, ways, offsets, interpret=False):
    tokens, columns = grads.shape
    hidden = weight.shape[0]
    width = hidden // ways
    tall = TALL
    extra = tall // GROUP

    def kernel(count_ref, mine_ref, grads_ref, *refs):
        step = pl.program_id(0)
        live = lax.broadcasted_iota(jnp.int32, (tall, width), 0) + step * tall < count_ref[0]
        for offset, part, out in zip(offsets, refs[: len(offsets)], refs[len(offsets) :]):
            share = lax.dot_general(
                grads_ref[...], part[...], (((1,), (1,)), ((), ())), preferred_element_type=f32
            )
            share = jnp.where(live, share, 0.0)
            if offset == 0:
                out[...] = share
                continue
            encode(share, out, 0)

    def part_of(offset):
        return pl.BlockSpec(
            (width, columns), lambda n, count, mine: (lax.rem(mine[0] + offset, ways), 0)
        )

    own = jax.ShapeDtypeStruct((tokens, width), f32)
    code = jax.ShapeDtypeStruct((tokens // tall, tall + extra, width), i16)
    own_spec = pl.BlockSpec((tall, width), lambda n, *_: (n, 0))
    code_spec = pl.BlockSpec((1, tall + extra, width), lambda n, *_: (n, 0, 0))
    return pl.pallas_call(
        kernel,
        grid_spec=pltpu.PrefetchScalarGridSpec(
            num_scalar_prefetch=2,
            grid=(tokens // tall,),
            in_specs=[pl.BlockSpec((tall, columns), lambda n, *_: (n, 0))]
            + [part_of(offset) for offset in offsets],
            out_specs=[own_spec if offset == 0 else code_spec for offset in offsets],
        ),
        out_shape=[own if offset == 0 else code for offset in offsets],
        compiler_params=pltpu.CompilerParams(vmem_limit_bytes=60 * 2**20),
        interpret=interpret,
    )(count, mine, grads, *[weight] * len(offsets))


def add_shares(own, coded, interpret=False):
    tokens, width = own.shape
    steps, padded, _ = coded[0].shape
    tall = tokens // steps
    groups = tall // GROUP

    def kernel(own_ref, *refs):
        out = refs[-1]

        def add(step, carry):
            base = pl.multiple_of(step * tall, tall)
            factors = [
                jnp.exp2(-ref[step, tall:padded, :].astype(jnp.int32).astype(f32))
                for ref in refs[:-1]
            ]
            for g in range(groups):
                rows = pl.ds(base + g * GROUP, GROUP)
                value = own_ref[rows, :]
                for ref, factor in zip(refs[:-1], factors):
                    code = ref[step, g * GROUP : (g + 1) * GROUP, :]
                    value += code.astype(jnp.int32).astype(f32) * factor[g : g + 1]
                out[rows, :] = value.astype(bf16)
            return carry

        lax.fori_loop(0, steps, add, 0)

    whole = pl.BlockSpec(memory_space=pltpu.VMEM)
    return pl.pallas_call(
        kernel,
        out_shape=jax.ShapeDtypeStruct((tokens, width), bf16),
        in_specs=[whole] * (1 + len(coded)),
        out_specs=whole,
        compiler_params=pltpu.CompilerParams(vmem_limit_bytes=12 * 2**20),
        interpret=interpret,
    )(own, *coded)


def place_blocks(pieces, owner_map, me, interpret=False):
    counts = [piece.shape[0] for piece in pieces]
    shape = (sum(counts), *pieces[0].shape[1:])

    def source_slot(position, me):
        core, zh, second, first = position // 32, (position // 16) % 2, (position // 4) % 4, position % 4
        far_x, far_y = (second, first) if zh else (first, second)
        x = lax.rem(lax.div(me, 8) + 4 - far_x, 4)
        y = lax.rem(lax.div(me, 2) + 4 - far_y, 4)
        my_zh, my_core = lax.div(me, 32), lax.rem(me, 2)
        return index_of(1 - my_zh if zh else my_zh, x, y, 1 - my_core if core else my_core)

    def kernel(map_ref, me_ref, *refs):
        sources, out, sent = refs[: len(pieces)], *refs[len(pieces) :]
        at = 0
        for source, count in zip(sources, counts):
            for b in range(count):
                row = map_ref[source_slot(at + b, me_ref[0])]
                pltpu.make_async_copy(source.at[b], out.at[row], sent).start()
            at += count
        pltpu.make_async_copy(out, out, sent).wait()

    return pl.pallas_call(
        kernel,
        out_shape=jax.ShapeDtypeStruct(shape, bf16),
        in_specs=[pl.BlockSpec(memory_space=pltpu.SMEM)] * 2
        + [pl.BlockSpec(memory_space=pltpu.VMEM)] * len(pieces),
        out_specs=pl.BlockSpec(memory_space=pl.ANY),
        scratch_shapes=[pltpu.SemaphoreType.DMA],
        compiler_params=pltpu.CompilerParams(vmem_limit_bytes=12 * 2**20),
        interpret=interpret,
    )(owner_map, me, *pieces)


def per_device(
    hidden_acts, out_grads, token_counts, down_weight, owner_map, master, moment1, moment2
):
    columns = out_grads.shape[1]
    hidden = hidden_acts.shape[1]
    me = lax.axis_index("dp").astype(jnp.int32).reshape(1)
    my_mp = lax.axis_index("mp").astype(jnp.int32).reshape(1)
    ways = lax.axis_size("mp")
    rings = (("x", "y"), ("y", "x"))

    def pass_share(coded, offset):
        ring = [(source, (source + offset) % ways) for source in range(ways)]
        return lax.ppermute(coded, "mp", ring)

    keep, send, up = weight_partials(
        hidden_acts, out_grads, down_weight, token_counts, owner_map, me, my_mp, ways
    )
    arrived = to_core(send)
    shares = [pass_share(up, 1)]
    states = jnp.stack([master, moment1, moment2.astype(f32)])
    other_states = to_zh(states)

    pair = [
        (keep[4 * i : 4 * i + 4].astype(f32) + arrived[4 * i : 4 * i + 4].astype(f32)).astype(bf16)
        for i in range(8)
    ]
    got = [
        [shift(pair[4 * colour + d], first, d) for d in (2, 1, 3)]
        for colour, (first, _) in enumerate(rings)
    ]
    got = lax.optimization_barrier(got)
    (down,) = input_shares(out_grads, down_weight, token_counts, my_mp, ways, (3,))
    shares.append(pass_share(down, 3))
    lines = [
        [
            sum((g[e].astype(f32) for g in got[colour]), pair[4 * colour][e].astype(f32)).astype(bf16)
            for e in range(4)
        ]
        for colour in range(2)
    ]
    got = [
        [shift(line[d], second, d) for d in (2, 1, 3)]
        for line, (_, second) in zip(lines, rings)
    ]
    got = lax.optimization_barrier(got)
    sums = [
        sum((g.astype(f32) for g in group), line[0].astype(f32)) for group, line in zip(got, lines)
    ]
    sums = lax.optimization_barrier(jnp.stack(sums))
    theirs = to_zh(sums)
    across, own = input_shares(out_grads, down_weight, token_counts, my_mp, ways, (2, 0))
    shares.append(pass_share(across, 2))

    summed = sums + theirs[::-1]
    digits = summed[:, :1, columns : columns + DIGITS]
    total = jnp.sum(digits * (4.0 ** jnp.arange(DIGITS, dtype=f32)), axis=(1, 2), keepdims=True)
    grad = summed[:, :, :columns] / total
    old_master, old_first, old_second = jnp.stack([states, other_states], axis=1)
    moment1_new = beta_one * old_first + (1.0 - beta_one) * grad
    second = beta_two * old_second + (1.0 - beta_two) * grad * grad
    master_new = old_master - learn_rate * (moment1_new / correct_one) / (
        jnp.sqrt(second / correct_two) + epsilon
    )
    weights = master_new.astype(bf16)
    master_new, moment1_new, moment2_new = master_new[0], moment1_new[0], second[0].astype(bf16)

    got = [
        [shift(weights[colour : colour + 1], first, d) for d in (2, 1, 3)]
        for colour, (first, _) in enumerate(rings)
    ]
    got = lax.optimization_barrier(got)
    pieces = []
    for colour, (_, second) in enumerate(rings):
        two, one, three = got[colour]
        line = jnp.concatenate([weights[colour : colour + 1], one, two, three])
        two, one, three = [shift(line, second, d) for d in (2, 1, 3)]
        pieces += [line, one, two, three]
    pieces += [to_core(piece) for piece in pieces]
    input_grads = add_shares(own, shares)
    weights_new = place_blocks(pieces, owner_map, me).reshape(hidden, columns)
    return (master_new, moment1_new, moment2_new, weights_new, input_grads)


def solution(mesh):
    in_specs = (
        P("dp", None),
        P("dp", "mp"),
        P("dp"),
        P(None, "mp"),
        P(),
        P("dp", "mp"),
        P("dp", "mp"),
        P("dp", "mp"),
    )
    out_specs = (P("dp", "mp"), P("dp", "mp"), P("dp", "mp"), P(None, "mp"), P("dp", "mp"))
    return jax.shard_map(per_device, mesh=mesh, in_specs=in_specs, out_specs=out_specs, check_vma=False)
```

```python
import jax
import jax.numpy as jnp
from jax import lax
from jax.experimental import pallas as pl
from jax.experimental.pallas import tpu as pltpu
from jax.sharding import PartitionSpec as P


beta_one = 0.9
beta_two = 0.95
learn_rate = 0.0003
epsilon = 1e-08
correct_one = 1.0 - 0.9**50
correct_two = 1.0 - 0.95**50


ZH, X, Y, CORE = 2, 4, 4, 2
f32, bf16, i16 = jnp.float32, jnp.bfloat16, jnp.int16
DIGITS = 6
EXTRA = 128
GROUP = 32


def index_of(zh, x, y, core):
    return ((zh * X + x) * Y + y) * CORE + core


def move(value, to):
    pairs = [
        (index_of(z, x, y, c), index_of(*to(z, x, y, c)))
        for z in range(ZH)
        for x in range(X)
        for y in range(Y)
        for c in range(CORE)
    ]
    return lax.ppermute(value, "dp", pairs)


def to_core(value):
    return move(value, lambda z, x, y, c: (z, x, y, 1 - c))


def to_zh(value):
    return move(value, lambda z, x, y, c: (1 - z, x, y, c))


def shift(value, ring, by):
    if ring == "x":
        return move(value, lambda z, x, y, c: (z, (x + by) % X, y, c))
    return move(value, lambda z, x, y, c: (z, x, (y + by) % Y, c))


def relative_slot(position, me):
    core, zh, first, second = position // 32, (position // 16) % 2, (position // 4) % 4, position % 4
    far_x, far_y = (second, first) if zh else (first, second)
    x = lax.rem(lax.div(me, 8) + far_x, 4)
    y = lax.rem(lax.div(me, 2) + far_y, 4)
    my_zh, my_core = lax.div(me, 32), lax.rem(me, 2)
    return index_of(1 - my_zh if zh else my_zh, x, y, 1 - my_core if core else my_core)


def encode(share, out, at):
    tall, width = share.shape
    groups = tall // GROUP
    largest = jnp.max(jnp.abs(share).reshape(groups, GROUP, width), axis=1)
    largest = jnp.max(largest, axis=1, keepdims=True)
    power = jnp.floor(jnp.log2(32000.0 / jnp.maximum(largest, 1e-25)))
    power = jnp.broadcast_to(jnp.minimum(power, 90.0), (groups, width))
    factor = jnp.exp2(power)
    for g in range(groups):
        code = jnp.round(share[g * GROUP : (g + 1) * GROUP] * factor[g : g + 1])
        out[at, g * GROUP : (g + 1) * GROUP, :] = code.astype(jnp.int32).astype(i16)
    out[at, tall : tall + groups, :] = power.astype(jnp.int32).astype(i16)


TALL = 512


def weight_partials(acts, grads, weight, count, owner_map, me, mine, ways, interpret=False):
    tokens, hidden = acts.shape
    columns = grads.shape[1]
    blocks = owner_map.shape[0]
    height = hidden // blocks
    wide = 512
    steps = columns // wide
    near = blocks // 2
    chunk = 512
    parts = tokens // chunk

    width = hidden // ways
    extra = TALL // GROUP

    def kernel(
        count_ref, map_ref, me_ref, mine_ref, acts_ref, grads_ref, weight_ref,
        keep_ref, send_ref, up_ref, raw, turned, part, total, sems,
    ):
        step = pl.program_id(0)

        def add_up():
            value = lax.dot_general(
                grads_ref[...], weight_ref[...], (((1,), (1,)), ((), ())), preferred_element_type=f32
            )

            @pl.when(step == 0)
            def _():
                total[...] = value

            @pl.when(step > 0)
            def _():
                total[...] += value

        def put():
            for p in range(blocks):
                start = pl.multiple_of(map_ref[relative_slot(p, me_ref[0])] * height, height)
                out = keep_ref if p < near else send_ref
                out[p % near] = part[pl.ds(start, height), :].astype(bf16)

        @pl.when(step == 0)
        def _():
            loads = [
                pltpu.make_async_copy(
                    acts_ref.at[pl.ds(i * chunk, chunk)], raw.at[pl.ds(i * chunk, chunk)], sems.at[i]
                )
                for i in range(parts)
            ]
            for load in loads:
                load.start()
            for i, load in enumerate(loads):
                rows = pl.ds(i * chunk, chunk)
                load.wait()
                live = lax.broadcasted_iota(jnp.int32, (1, chunk), 1) + i * chunk < count_ref[0]
                flipped = raw[rows, :].T * jnp.where(live, 1.0, 0.0).astype(bf16)
                turned[:, rows] = flipped
                value = jnp.dot(flipped, grads_ref[rows, :], preferred_element_type=f32)
                if i == 0:
                    part[...] = value
                else:
                    part[...] += value
            put()
            add_up()

        @pl.when((step > 0) & (step < steps))
        def _():
            part[...] = jnp.dot(turned[...], grads_ref[...], preferred_element_type=f32)
            put()
            add_up()

        @pl.when(step == steps)
        def _():
            lane = lax.broadcasted_iota(jnp.int32, (near, height, EXTRA), 2)
            digit = (count_ref[0] >> jnp.minimum(2 * lane, 30)) & 3
            value = digit.astype(f32).astype(bf16)
            keep_ref[:, :, :EXTRA] = value
            send_ref[:, :, :EXTRA] = value
            for i in range(tokens // TALL):
                live = lax.broadcasted_iota(jnp.int32, (TALL, width), 0) + i * TALL < count_ref[0]
                encode(jnp.where(live, total[i * TALL : (i + 1) * TALL], 0.0), up_ref, i)

    out = jax.ShapeDtypeStruct((near, height, columns + EXTRA), bf16)
    spec = pl.BlockSpec((near, height, wide), lambda n, *_: (0, 0, n))
    code = (tokens // TALL, TALL + extra, width)
    return pl.pallas_call(
        kernel,
        grid_spec=pltpu.PrefetchScalarGridSpec(
            num_scalar_prefetch=4,
            grid=(steps + 1,),
            in_specs=[
                pl.BlockSpec(memory_space=pl.ANY),
                pl.BlockSpec((tokens, wide), lambda n, *_: (0, jnp.minimum(n, steps - 1))),
                pl.BlockSpec(
                    (width, wide),
                    lambda n, count, map, me, mine: (
                        lax.rem(mine[0] + 1, ways),
                        jnp.minimum(n, steps - 1),
                    ),
                ),
            ],
            out_specs=[spec, spec, pl.BlockSpec(code, lambda n, *_: (0, 0, 0))],
            scratch_shapes=[
                pltpu.VMEM((tokens, hidden), bf16),
                pltpu.VMEM((hidden, tokens), bf16),
                pltpu.VMEM((hidden, wide), f32),
                pltpu.VMEM((tokens, width), f32),
                pltpu.SemaphoreType.DMA((parts,)),
            ],
        ),
        out_shape=[out, out, jax.ShapeDtypeStruct(code, i16)],
        compiler_params=pltpu.CompilerParams(vmem_limit_bytes=60 * 2**20),
        interpret=interpret,
    )(count, owner_map, me, mine, acts, grads, weight)


def input_shares(grads, weight, count, mine, ways, offsets, interpret=False):
    tokens, columns = grads.shape
    hidden = weight.shape[0]
    width = hidden // ways
    tall = TALL
    extra = tall // GROUP

    def kernel(count_ref, mine_ref, grads_ref, *refs):
        step = pl.program_id(0)
        live = lax.broadcasted_iota(jnp.int32, (tall, width), 0) + step * tall < count_ref[0]
        for offset, part, out in zip(offsets, refs[: len(offsets)], refs[len(offsets) :]):
            share = lax.dot_general(
                grads_ref[...], part[...], (((1,), (1,)), ((), ())), preferred_element_type=f32
            )
            share = jnp.where(live, share, 0.0)
            if offset == 0:
                out[...] = share
                continue
            encode(share, out, 0)

    def part_of(offset):
        return pl.BlockSpec(
            (width, columns), lambda n, count, mine: (lax.rem(mine[0] + offset, ways), 0)
        )

    own = jax.ShapeDtypeStruct((tokens, width), f32)
    code = jax.ShapeDtypeStruct((tokens // tall, tall + extra, width), i16)
    own_spec = pl.BlockSpec((tall, width), lambda n, *_: (n, 0))
    code_spec = pl.BlockSpec((1, tall + extra, width), lambda n, *_: (n, 0, 0))
    return pl.pallas_call(
        kernel,
        grid_spec=pltpu.PrefetchScalarGridSpec(
            num_scalar_prefetch=2,
            grid=(tokens // tall,),
            in_specs=[pl.BlockSpec((tall, columns), lambda n, *_: (n, 0))]
            + [part_of(offset) for offset in offsets],
            out_specs=[own_spec if offset == 0 else code_spec for offset in offsets],
        ),
        out_shape=[own if offset == 0 else code for offset in offsets],
        compiler_params=pltpu.CompilerParams(vmem_limit_bytes=60 * 2**20),
        interpret=interpret,
    )(count, mine, grads, *[weight] * len(offsets))


def add_shares(own, coded, interpret=False):
    tokens, width = own.shape
    steps, padded, _ = coded[0].shape
    tall = tokens // steps
    groups = tall // GROUP

    def kernel(own_ref, *refs):
        out = refs[-1]

        def add(step, carry):
            base = pl.multiple_of(step * tall, tall)
            factors = [
                jnp.exp2(-ref[step, tall:padded, :].astype(jnp.int32).astype(f32))
                for ref in refs[:-1]
            ]
            for g in range(groups):
                rows = pl.ds(base + g * GROUP, GROUP)
                value = own_ref[rows, :]
                for ref, factor in zip(refs[:-1], factors):
                    code = ref[step, g * GROUP : (g + 1) * GROUP, :]
                    value += code.astype(jnp.int32).astype(f32) * factor[g : g + 1]
                out[rows, :] = value.astype(bf16)
            return carry

        lax.fori_loop(0, steps, add, 0)

    whole = pl.BlockSpec(memory_space=pltpu.VMEM)
    return pl.pallas_call(
        kernel,
        out_shape=jax.ShapeDtypeStruct((tokens, width), bf16),
        in_specs=[whole] * (1 + len(coded)),
        out_specs=whole,
        compiler_params=pltpu.CompilerParams(vmem_limit_bytes=12 * 2**20),
        interpret=interpret,
    )(own, *coded)


def place_blocks(pieces, owner_map, me, interpret=False):
    counts = [piece.shape[0] for piece in pieces]
    shape = (sum(counts), *pieces[0].shape[1:])

    def source_slot(position, me):
        core, zh, second, first = position // 32, (position // 16) % 2, (position // 4) % 4, position % 4
        far_x, far_y = (second, first) if zh else (first, second)
        x = lax.rem(lax.div(me, 8) + 4 - far_x, 4)
        y = lax.rem(lax.div(me, 2) + 4 - far_y, 4)
        my_zh, my_core = lax.div(me, 32), lax.rem(me, 2)
        return index_of(1 - my_zh if zh else my_zh, x, y, 1 - my_core if core else my_core)

    def kernel(map_ref, me_ref, *refs):
        sources, out, sent = refs[: len(pieces)], *refs[len(pieces) :]
        at = 0
        for source, count in zip(sources, counts):
            for b in range(count):
                row = map_ref[source_slot(at + b, me_ref[0])]
                pltpu.make_async_copy(source.at[b], out.at[row], sent).start()
            at += count
        pltpu.make_async_copy(out, out, sent).wait()

    return pl.pallas_call(
        kernel,
        out_shape=jax.ShapeDtypeStruct(shape, bf16),
        in_specs=[pl.BlockSpec(memory_space=pltpu.SMEM)] * 2
        + [pl.BlockSpec(memory_space=pltpu.VMEM)] * len(pieces),
        out_specs=pl.BlockSpec(memory_space=pl.ANY),
        scratch_shapes=[pltpu.SemaphoreType.DMA],
        compiler_params=pltpu.CompilerParams(vmem_limit_bytes=12 * 2**20),
        interpret=interpret,
    )(owner_map, me, *pieces)


def per_device(
    hidden_acts, out_grads, token_counts, down_weight, owner_map, master, moment1, moment2
):
    columns = out_grads.shape[1]
    hidden = hidden_acts.shape[1]
    me = lax.axis_index("dp").astype(jnp.int32).reshape(1)
    my_mp = lax.axis_index("mp").astype(jnp.int32).reshape(1)
    ways = lax.axis_size("mp")
    rings = (("x", "y"), ("y", "x"))

    def pass_share(coded, offset):
        ring = [(source, (source + offset) % ways) for source in range(ways)]
        return lax.ppermute(coded, "mp", ring)

    keep, send, up = weight_partials(
        hidden_acts, out_grads, down_weight, token_counts, owner_map, me, my_mp, ways
    )
    arrived = to_core(send)
    shares = [pass_share(up, 1)]
    (down,) = input_shares(out_grads, down_weight, token_counts, my_mp, ways, (3,))
    shares.append(pass_share(down, 3))
    pair = [
        (keep[4 * i : 4 * i + 4].astype(f32) + arrived[4 * i : 4 * i + 4].astype(f32)).astype(bf16)
        for i in range(8)
    ]
    got = [
        [shift(pair[4 * colour + d], first, d) for d in (2, 1, 3)]
        for colour, (first, _) in enumerate(rings)
    ]
    got = lax.optimization_barrier(got)
    lines = [
        [
            sum((g[e].astype(f32) for g in got[colour]), pair[4 * colour][e].astype(f32)).astype(bf16)
            for e in range(4)
        ]
        for colour in range(2)
    ]
    got = [
        [shift(line[d], second, d) for d in (2, 1, 3)]
        for line, (_, second) in zip(lines, rings)
    ]
    got = lax.optimization_barrier(got)
    sums = [
        sum((g.astype(f32) for g in group), line[0].astype(f32)) for group, line in zip(got, lines)
    ]
    theirs = to_zh(sums[1])
    across, own = input_shares(out_grads, down_weight, token_counts, my_mp, ways, (2, 0))
    summed = sums[0] + theirs

    digits = summed[:1, columns : columns + DIGITS]
    total = jnp.sum(digits * (4.0 ** jnp.arange(DIGITS, dtype=f32)))
    grad = summed[:, :columns] / total
    moment1_new = beta_one * moment1 + (1.0 - beta_one) * grad
    second = beta_two * moment2.astype(f32) + (1.0 - beta_two) * grad * grad
    moment2_new = second.astype(bf16)
    master_new = master - learn_rate * (moment1_new / correct_one) / (
        jnp.sqrt(second / correct_two) + epsilon
    )

    weights = master_new.astype(bf16)[None]
    other = to_zh(weights)
    shares.append(pass_share(across, 2))
    lines = []
    for part, (first, _) in zip((weights, other), rings):
        two, one, three = [shift(part, first, d) for d in (2, 1, 3)]
        lines.append(jnp.concatenate([part, one, two, three]))
    pieces = []
    for line, (_, second) in zip(lines, rings):
        two, one, three = [shift(line, second, d) for d in (2, 1, 3)]
        pieces += [line, one, two, three]
    pieces += [to_core(piece) for piece in pieces]
    input_grads = add_shares(own, shares)
    weights_new = place_blocks(pieces, owner_map, me).reshape(hidden, columns)
    return (master_new, moment1_new, moment2_new, weights_new, input_grads)


def solution(mesh):
    in_specs = (
        P("dp", None),
        P("dp", "mp"),
        P("dp"),
        P(None, "mp"),
        P(),
        P("dp", "mp"),
        P("dp", "mp"),
        P("dp", "mp"),
    )
    out_specs = (P("dp", "mp"), P("dp", "mp"), P("dp", "mp"), P(None, "mp"), P("dp", "mp"))
    return jax.shard_map(per_device, mesh=mesh, in_specs=in_specs, out_specs=out_specs, check_vma=False)
```

```python
import jax
import jax.numpy as jnp
from jax import lax
from jax.experimental import pallas as pl
from jax.experimental.pallas import tpu as pltpu
from jax.sharding import PartitionSpec as P


beta_one = 0.9
beta_two = 0.95
learn_rate = 0.0003
epsilon = 1e-08
correct_one = 1.0 - 0.9**50
correct_two = 1.0 - 0.95**50


ZH, X, Y, CORE = 2, 4, 4, 2
f32, bf16, i16 = jnp.float32, jnp.bfloat16, jnp.int16
DIGITS = 6
EXTRA = 128
GROUP = 32


def index_of(zh, x, y, core):
    return ((zh * X + x) * Y + y) * CORE + core


def move(value, to):
    pairs = [
        (index_of(z, x, y, c), index_of(*to(z, x, y, c)))
        for z in range(ZH)
        for x in range(X)
        for y in range(Y)
        for c in range(CORE)
    ]
    return lax.ppermute(value, "dp", pairs)


def to_core(value):
    return move(value, lambda z, x, y, c: (z, x, y, 1 - c))


def to_zh(value):
    return move(value, lambda z, x, y, c: (1 - z, x, y, c))


def shift(value, ring, by):
    if ring == "x":
        return move(value, lambda z, x, y, c: (z, (x + by) % X, y, c))
    return move(value, lambda z, x, y, c: (z, x, (y + by) % Y, c))


def relative_slot(position, me):
    core, zh, first, second = position // 32, (position // 16) % 2, (position // 4) % 4, position % 4
    far_x, far_y = (second, first) if zh else (first, second)
    x = lax.rem(lax.div(me, 8) + far_x, 4)
    y = lax.rem(lax.div(me, 2) + far_y, 4)
    my_zh, my_core = lax.div(me, 32), lax.rem(me, 2)
    return index_of(1 - my_zh if zh else my_zh, x, y, 1 - my_core if core else my_core)


def encode(share, out, at):
    tall, width = share.shape
    groups = tall // GROUP
    largest = jnp.max(jnp.abs(share).reshape(groups, GROUP, width), axis=1)
    largest = jnp.max(largest, axis=1, keepdims=True)
    power = jnp.floor(jnp.log2(32000.0 / jnp.maximum(largest, 1e-25)))
    power = jnp.broadcast_to(jnp.minimum(power, 90.0), (groups, width))
    factor = jnp.exp2(power)
    for g in range(groups):
        code = jnp.round(share[g * GROUP : (g + 1) * GROUP] * factor[g : g + 1])
        out[at, g * GROUP : (g + 1) * GROUP, :] = code.astype(jnp.int32).astype(i16)
    out[at, tall : tall + groups, :] = power.astype(jnp.int32).astype(i16)


TALL = 512


def weight_partials(acts, grads, weight, count, owner_map, me, mine, ways, interpret=False):
    tokens, hidden = acts.shape
    columns = grads.shape[1]
    blocks = owner_map.shape[0]
    height = hidden // blocks
    wide = 512
    steps = columns // wide
    near = blocks // 2
    chunk = 512
    parts = tokens // chunk

    width = hidden // ways
    extra = TALL // GROUP

    def kernel(
        count_ref, map_ref, me_ref, mine_ref, acts_ref, grads_ref, up_part_ref, down_part_ref,
        keep_ref, send_ref, up_ref, down_ref, raw, turned, part, up_sum, down_sum, sems,
    ):
        step = pl.program_id(0)

        def add_shares_of(first):
            for weight_ref, total in ((up_part_ref, up_sum), (down_part_ref, down_sum)):
                value = lax.dot_general(
                    grads_ref[...],
                    weight_ref[...],
                    (((1,), (1,)), ((), ())),
                    preferred_element_type=f32,
                )
                total[...] = value if first else total[...] + value

        def put():
            for p in range(blocks):
                start = pl.multiple_of(map_ref[relative_slot(p, me_ref[0])] * height, height)
                out = keep_ref if p < near else send_ref
                out[p % near] = part[pl.ds(start, height), :].astype(bf16)

        @pl.when(step == 0)
        def _():
            loads = [
                pltpu.make_async_copy(
                    acts_ref.at[pl.ds(i * chunk, chunk)], raw.at[pl.ds(i * chunk, chunk)], sems.at[i]
                )
                for i in range(parts)
            ]
            for load in loads:
                load.start()
            for i, load in enumerate(loads):
                rows = pl.ds(i * chunk, chunk)
                load.wait()
                live = lax.broadcasted_iota(jnp.int32, (1, chunk), 1) + i * chunk < count_ref[0]
                flipped = raw[rows, :].T * jnp.where(live, 1.0, 0.0).astype(bf16)
                turned[:, rows] = flipped
                value = jnp.dot(flipped, grads_ref[rows, :], preferred_element_type=f32)
                if i == 0:
                    part[...] = value
                else:
                    part[...] += value
            put()
            add_shares_of(True)

        @pl.when((step > 0) & (step < steps))
        def _():
            part[...] = jnp.dot(turned[...], grads_ref[...], preferred_element_type=f32)
            put()
            add_shares_of(False)

        @pl.when(step == steps)
        def _():
            lane = lax.broadcasted_iota(jnp.int32, (near, height, EXTRA), 2)
            digit = (count_ref[0] >> jnp.minimum(2 * lane, 30)) & 3
            value = digit.astype(f32).astype(bf16)
            keep_ref[:, :, :EXTRA] = value
            send_ref[:, :, :EXTRA] = value
            for i in range(tokens // TALL):
                live = lax.broadcasted_iota(jnp.int32, (TALL, width), 0) + i * TALL < count_ref[0]
                for total, coded_ref in ((up_sum, up_ref), (down_sum, down_ref)):
                    encode(jnp.where(live, total[i * TALL : (i + 1) * TALL], 0.0), coded_ref, i)

    out = jax.ShapeDtypeStruct((near, height, columns + EXTRA), bf16)
    spec = pl.BlockSpec((near, height, wide), lambda n, *_: (0, 0, n))
    code = (tokens // TALL, TALL + extra, width)

    def part_of(offset):
        return pl.BlockSpec(
            (width, wide),
            lambda n, count, map, me, mine: (
                lax.rem(mine[0] + offset, ways),
                jnp.minimum(n, steps - 1),
            ),
        )

    return pl.pallas_call(
        kernel,
        grid_spec=pltpu.PrefetchScalarGridSpec(
            num_scalar_prefetch=4,
            grid=(steps + 1,),
            in_specs=[
                pl.BlockSpec(memory_space=pl.ANY),
                pl.BlockSpec((tokens, wide), lambda n, *_: (0, jnp.minimum(n, steps - 1))),
                part_of(1),
                part_of(ways - 1),
            ],
            out_specs=[spec, spec] + [pl.BlockSpec(code, lambda n, *_: (0, 0, 0))] * 2,
            scratch_shapes=[
                pltpu.VMEM((tokens, hidden), bf16),
                pltpu.VMEM((hidden, tokens), bf16),
                pltpu.VMEM((hidden, wide), f32),
                pltpu.VMEM((tokens, width), f32),
                pltpu.VMEM((tokens, width), f32),
                pltpu.SemaphoreType.DMA((parts,)),
            ],
        ),
        out_shape=[out, out] + [jax.ShapeDtypeStruct(code, i16)] * 2,
        compiler_params=pltpu.CompilerParams(vmem_limit_bytes=60 * 2**20),
        interpret=interpret,
    )(count, owner_map, me, mine, acts, grads, weight, weight)


def input_shares(grads, weight, count, mine, ways, offsets, interpret=False):
    tokens, columns = grads.shape
    hidden = weight.shape[0]
    width = hidden // ways
    tall = TALL
    extra = tall // GROUP

    def kernel(count_ref, mine_ref, grads_ref, *refs):
        step = pl.program_id(0)
        live = lax.broadcasted_iota(jnp.int32, (tall, width), 0) + step * tall < count_ref[0]
        for offset, part, out in zip(offsets, refs[: len(offsets)], refs[len(offsets) :]):
            share = lax.dot_general(
                grads_ref[...], part[...], (((1,), (1,)), ((), ())), preferred_element_type=f32
            )
            share = jnp.where(live, share, 0.0)
            if offset == 0:
                out[...] = share
                continue
            encode(share, out, 0)

    def part_of(offset):
        return pl.BlockSpec(
            (width, columns), lambda n, count, mine: (lax.rem(mine[0] + offset, ways), 0)
        )

    own = jax.ShapeDtypeStruct((tokens, width), f32)
    code = jax.ShapeDtypeStruct((tokens // tall, tall + extra, width), i16)
    own_spec = pl.BlockSpec((tall, width), lambda n, *_: (n, 0))
    code_spec = pl.BlockSpec((1, tall + extra, width), lambda n, *_: (n, 0, 0))
    return pl.pallas_call(
        kernel,
        grid_spec=pltpu.PrefetchScalarGridSpec(
            num_scalar_prefetch=2,
            grid=(tokens // tall,),
            in_specs=[pl.BlockSpec((tall, columns), lambda n, *_: (n, 0))]
            + [part_of(offset) for offset in offsets],
            out_specs=[own_spec if offset == 0 else code_spec for offset in offsets],
        ),
        out_shape=[own if offset == 0 else code for offset in offsets],
        compiler_params=pltpu.CompilerParams(vmem_limit_bytes=60 * 2**20),
        interpret=interpret,
    )(count, mine, grads, *[weight] * len(offsets))


def add_shares(own, shares, interpret=False):
    tokens, width = own.shape
    places = [[(i, j) for i, piece in enumerate(share) for j in range(piece.shape[0])] for share in shares]
    steps = len(places[0])
    tall = tokens // steps
    groups = tall // GROUP
    pieces = [piece for share in shares for piece in share]

    def kernel(own_ref, *refs):
        out, refs = refs[-1], list(refs[:-1])
        held = [[refs.pop(0) for _ in share] for share in shares]
        for step in range(steps):
            blocks = [mine[places[k][step][0]].at[places[k][step][1]] for k, mine in enumerate(held)]
            factors = [
                jnp.exp2(-block[tall : tall + groups, :].astype(jnp.int32).astype(f32))
                for block in blocks
            ]
            for g in range(groups):
                rows = slice(step * tall + g * GROUP, step * tall + (g + 1) * GROUP)
                value = own_ref[rows, :]
                for block, factor in zip(blocks, factors):
                    code = block[g * GROUP : (g + 1) * GROUP, :]
                    value += code.astype(jnp.int32).astype(f32) * factor[g : g + 1]
                out[rows, :] = value.astype(bf16)

    whole = pl.BlockSpec(memory_space=pltpu.VMEM)
    return pl.pallas_call(
        kernel,
        out_shape=jax.ShapeDtypeStruct((tokens, width), bf16),
        in_specs=[whole] * (1 + len(pieces)),
        out_specs=whole,
        compiler_params=pltpu.CompilerParams(vmem_limit_bytes=12 * 2**20),
        interpret=interpret,
    )(own, *pieces)


def place_blocks(pieces, owner_map, me, interpret=False):
    counts = [piece.shape[0] for piece in pieces]
    shape = (sum(counts), *pieces[0].shape[1:])

    def source_slot(position, me):
        core, zh, second, first = position // 32, (position // 16) % 2, (position // 4) % 4, position % 4
        far_x, far_y = (second, first) if zh else (first, second)
        x = lax.rem(lax.div(me, 8) + 4 - far_x, 4)
        y = lax.rem(lax.div(me, 2) + 4 - far_y, 4)
        my_zh, my_core = lax.div(me, 32), lax.rem(me, 2)
        return index_of(1 - my_zh if zh else my_zh, x, y, 1 - my_core if core else my_core)

    def kernel(map_ref, me_ref, *refs):
        sources, out, sent = refs[: len(pieces)], *refs[len(pieces) :]
        at = 0
        for source, count in zip(sources, counts):
            for b in range(count):
                row = map_ref[source_slot(at + b, me_ref[0])]
                pltpu.make_async_copy(source.at[b], out.at[row], sent).start()
            at += count
        pltpu.make_async_copy(out, out, sent).wait()

    return pl.pallas_call(
        kernel,
        out_shape=jax.ShapeDtypeStruct(shape, bf16),
        in_specs=[pl.BlockSpec(memory_space=pltpu.SMEM)] * 2
        + [pl.BlockSpec(memory_space=pltpu.VMEM)] * len(pieces),
        out_specs=pl.BlockSpec(memory_space=pl.ANY),
        scratch_shapes=[pltpu.SemaphoreType.DMA],
        compiler_params=pltpu.CompilerParams(vmem_limit_bytes=12 * 2**20),
        interpret=interpret,
    )(owner_map, me, *pieces)


def per_device(
    hidden_acts, out_grads, token_counts, down_weight, owner_map, master, moment1, moment2
):
    columns = out_grads.shape[1]
    hidden = hidden_acts.shape[1]
    me = lax.axis_index("dp").astype(jnp.int32).reshape(1)
    my_mp = lax.axis_index("mp").astype(jnp.int32).reshape(1)
    ways = lax.axis_size("mp")
    rings = (("x", "y"), ("y", "x"))

    def pass_share(coded, offset):
        ring = [(source, (source + offset) % ways) for source in range(ways)]
        return lax.ppermute(coded, "mp", ring)

    keep, send, up, down = weight_partials(
        hidden_acts, out_grads, down_weight, token_counts, owner_map, me, my_mp, ways
    )
    arrived = to_core(send)
    shares = [[pass_share(up, 1)], [pass_share(down, 3)]]
    arrived, far_grads = lax.optimization_barrier((arrived, out_grads))
    pair = [
        (keep[4 * i : 4 * i + 4].astype(f32) + arrived[4 * i : 4 * i + 4].astype(f32)).astype(bf16)
        for i in range(8)
    ]
    got = [
        [shift(pair[4 * colour + d], first, d) for d in (2, 1, 3)]
        for colour, (first, _) in enumerate(rings)
    ]
    got = lax.optimization_barrier(got)
    across, own = input_shares(far_grads, down_weight, token_counts, my_mp, ways, (2, 0))
    across_early = pass_share(across[:1], 2)
    lines = [
        [
            sum((g[e].astype(f32) for g in got[colour]), pair[4 * colour][e].astype(f32)).astype(bf16)
            for e in range(4)
        ]
        for colour in range(2)
    ]
    got = [
        [shift(line[d], second, d) for d in (2, 1, 3)]
        for line, (_, second) in zip(lines, rings)
    ]
    got, across_rest = lax.optimization_barrier((got, across[1:]))
    sums = [
        sum((g.astype(f32) for g in group), line[0].astype(f32)) for group, line in zip(got, lines)
    ]
    theirs = to_zh(sums[1])
    summed = sums[0] + theirs

    digits = summed[:1, columns : columns + DIGITS]
    total = jnp.sum(digits * (4.0 ** jnp.arange(DIGITS, dtype=f32)))
    grad = summed[:, :columns] / total
    moment1_new = beta_one * moment1 + (1.0 - beta_one) * grad
    second = beta_two * moment2.astype(f32) + (1.0 - beta_two) * grad * grad
    moment2_new = second.astype(bf16)
    master_new = master - learn_rate * (moment1_new / correct_one) / (
        jnp.sqrt(second / correct_two) + epsilon
    )

    weights = master_new.astype(bf16)[None]
    other = to_zh(weights)
    shares.append([across_early, pass_share(across_rest, 2)])
    lines = []
    for part, (first, _) in zip((weights, other), rings):
        two, one, three = [shift(part, first, d) for d in (2, 1, 3)]
        lines.append(jnp.concatenate([part, one, two, three]))
    pieces = []
    for line, (_, second) in zip(lines, rings):
        two, one, three = [shift(line, second, d) for d in (2, 1, 3)]
        pieces += [line, one, two, three]
    pieces += [to_core(piece) for piece in pieces]
    input_grads = add_shares(own, shares)
    weights_new = place_blocks(pieces, owner_map, me).reshape(hidden, columns)
    return (master_new, moment1_new, moment2_new, weights_new, input_grads)


def solution(mesh):
    in_specs = (
        P("dp", None),
        P("dp", "mp"),
        P("dp"),
        P(None, "mp"),
        P(),
        P("dp", "mp"),
        P("dp", "mp"),
        P("dp", "mp"),
    )
    out_specs = (P("dp", "mp"), P("dp", "mp"), P("dp", "mp"), P(None, "mp"), P("dp", "mp"))
    return jax.shard_map(per_device, mesh=mesh, in_specs=in_specs, out_specs=out_specs, check_vma=False)
```

```python
import jax
import jax.numpy as jnp
from jax import lax
from jax.experimental import pallas as pl
from jax.experimental.pallas import tpu as pltpu
from jax.sharding import PartitionSpec as P


beta_one = 0.9
beta_two = 0.95
learn_rate = 0.0003
epsilon = 1e-08
correct_one = 1.0 - 0.9**50
correct_two = 1.0 - 0.95**50


ZH, X, Y, CORE = 2, 4, 4, 2
f32, bf16, i16 = jnp.float32, jnp.bfloat16, jnp.int16
DIGITS = 6
EXTRA = 128
GROUP = 32


def index_of(zh, x, y, core):
    return ((zh * X + x) * Y + y) * CORE + core


def move(value, to):
    pairs = [
        (index_of(z, x, y, c), index_of(*to(z, x, y, c)))
        for z in range(ZH)
        for x in range(X)
        for y in range(Y)
        for c in range(CORE)
    ]
    return lax.ppermute(value, "dp", pairs)


def to_core(value):
    return move(value, lambda z, x, y, c: (z, x, y, 1 - c))


def to_zh(value):
    return move(value, lambda z, x, y, c: (1 - z, x, y, c))


def shift(value, ring, by):
    if ring == "x":
        return move(value, lambda z, x, y, c: (z, (x + by) % X, y, c))
    return move(value, lambda z, x, y, c: (z, x, (y + by) % Y, c))


def relative_slot(position, me):
    core, zh, first, second = position // 32, (position // 16) % 2, (position // 4) % 4, position % 4
    far_x, far_y = (second, first) if zh else (first, second)
    x = lax.rem(lax.div(me, 8) + far_x, 4)
    y = lax.rem(lax.div(me, 2) + far_y, 4)
    my_zh, my_core = lax.div(me, 32), lax.rem(me, 2)
    return index_of(1 - my_zh if zh else my_zh, x, y, 1 - my_core if core else my_core)


def encode(share, out, at):
    tall, width = share.shape
    groups = tall // GROUP
    largest = jnp.max(jnp.abs(share).reshape(groups, GROUP, width), axis=1)
    largest = jnp.max(largest, axis=1, keepdims=True)
    power = jnp.floor(jnp.log2(32000.0 / jnp.maximum(largest, 1e-25)))
    power = jnp.broadcast_to(jnp.minimum(power, 90.0), (groups, width))
    factor = jnp.exp2(power)
    for g in range(groups):
        code = jnp.round(share[g * GROUP : (g + 1) * GROUP] * factor[g : g + 1])
        out[at, g * GROUP : (g + 1) * GROUP, :] = code.astype(jnp.int32).astype(i16)
    out[at, tall : tall + groups, :] = power.astype(jnp.int32).astype(i16)


TALL = 512


def weight_partials(acts, grads, weight, count, owner_map, me, mine, ways, interpret=False):
    tokens, hidden = acts.shape
    columns = grads.shape[1]
    blocks = owner_map.shape[0]
    height = hidden // blocks
    wide = 512
    steps = columns // wide
    near = blocks // 2
    chunk = 512
    parts = tokens // chunk

    width = hidden // ways
    extra = TALL // GROUP

    def kernel(
        count_ref, map_ref, me_ref, mine_ref, acts_ref, grads_ref, up_part_ref, down_part_ref,
        keep_ref, send_ref, up_ref, down_ref, raw, turned, part, up_sum, down_sum, sems,
    ):
        step = pl.program_id(0)

        def add_shares_of(first):
            for weight_ref, total in ((up_part_ref, up_sum), (down_part_ref, down_sum)):
                value = lax.dot_general(
                    grads_ref[...],
                    weight_ref[...],
                    (((1,), (1,)), ((), ())),
                    preferred_element_type=f32,
                )
                total[...] = value if first else total[...] + value

        def put():
            for p in range(blocks):
                start = pl.multiple_of(map_ref[relative_slot(p, me_ref[0])] * height, height)
                out = keep_ref if p < near else send_ref
                out[p % near] = part[pl.ds(start, height), :].astype(bf16)

        @pl.when(step == 0)
        def _():
            loads = [
                pltpu.make_async_copy(
                    acts_ref.at[pl.ds(i * chunk, chunk)], raw.at[pl.ds(i * chunk, chunk)], sems.at[i]
                )
                for i in range(parts)
            ]
            for load in loads:
                load.start()
            for i, load in enumerate(loads):
                rows = pl.ds(i * chunk, chunk)
                load.wait()
                live = lax.broadcasted_iota(jnp.int32, (1, chunk), 1) + i * chunk < count_ref[0]
                flipped = raw[rows, :].T * jnp.where(live, 1.0, 0.0).astype(bf16)
                turned[:, rows] = flipped
                value = jnp.dot(flipped, grads_ref[rows, :], preferred_element_type=f32)
                if i == 0:
                    part[...] = value
                else:
                    part[...] += value
            put()
            add_shares_of(True)

        @pl.when((step > 0) & (step < steps))
        def _():
            part[...] = jnp.dot(turned[...], grads_ref[...], preferred_element_type=f32)
            put()
            add_shares_of(False)

        @pl.when(step == steps)
        def _():
            lane = lax.broadcasted_iota(jnp.int32, (near, height, EXTRA), 2)
            digit = (count_ref[0] >> jnp.minimum(2 * lane, 30)) & 3
            value = digit.astype(f32).astype(bf16)
            keep_ref[:, :, :EXTRA] = value
            send_ref[:, :, :EXTRA] = value
            for i in range(tokens // TALL):
                live = lax.broadcasted_iota(jnp.int32, (TALL, width), 0) + i * TALL < count_ref[0]
                for total, coded_ref in ((up_sum, up_ref), (down_sum, down_ref)):
                    encode(jnp.where(live, total[i * TALL : (i + 1) * TALL], 0.0), coded_ref, i)

    out = jax.ShapeDtypeStruct((near, height, columns + EXTRA), bf16)
    spec = pl.BlockSpec((near, height, wide), lambda n, *_: (0, 0, n))
    code = (tokens // TALL, TALL + extra, width)

    def part_of(offset):
        return pl.BlockSpec(
            (width, wide),
            lambda n, count, map, me, mine: (
                lax.rem(mine[0] + offset, ways),
                jnp.minimum(n, steps - 1),
            ),
        )

    return pl.pallas_call(
        kernel,
        grid_spec=pltpu.PrefetchScalarGridSpec(
            num_scalar_prefetch=4,
            grid=(steps + 1,),
            in_specs=[
                pl.BlockSpec(memory_space=pl.ANY),
                pl.BlockSpec((tokens, wide), lambda n, *_: (0, jnp.minimum(n, steps - 1))),
                part_of(1),
                part_of(ways - 1),
            ],
            out_specs=[spec, spec] + [pl.BlockSpec(code, lambda n, *_: (0, 0, 0))] * 2,
            scratch_shapes=[
                pltpu.VMEM((tokens, hidden), bf16),
                pltpu.VMEM((hidden, tokens), bf16),
                pltpu.VMEM((hidden, wide), f32),
                pltpu.VMEM((tokens, width), f32),
                pltpu.VMEM((tokens, width), f32),
                pltpu.SemaphoreType.DMA((parts,)),
            ],
        ),
        out_shape=[out, out] + [jax.ShapeDtypeStruct(code, i16)] * 2,
        compiler_params=pltpu.CompilerParams(vmem_limit_bytes=60 * 2**20),
        interpret=interpret,
    )(count, owner_map, me, mine, acts, grads, weight, weight)


def input_shares(grads, weight, count, mine, ways, offsets, interpret=False):
    tokens, columns = grads.shape
    hidden = weight.shape[0]
    width = hidden // ways
    tall = TALL
    extra = tall // GROUP

    def kernel(count_ref, mine_ref, grads_ref, *refs):
        step = pl.program_id(0)
        live = lax.broadcasted_iota(jnp.int32, (tall, width), 0) + step * tall < count_ref[0]
        for offset, part, out in zip(offsets, refs[: len(offsets)], refs[len(offsets) :]):
            share = lax.dot_general(
                grads_ref[...], part[...], (((1,), (1,)), ((), ())), preferred_element_type=f32
            )
            share = jnp.where(live, share, 0.0)
            if offset == 0:
                out[...] = share
                continue
            encode(share, out, 0)

    def part_of(offset):
        return pl.BlockSpec(
            (width, columns), lambda n, count, mine: (lax.rem(mine[0] + offset, ways), 0)
        )

    own = jax.ShapeDtypeStruct((tokens, width), f32)
    code = jax.ShapeDtypeStruct((tokens // tall, tall + extra, width), i16)
    own_spec = pl.BlockSpec((tall, width), lambda n, *_: (n, 0))
    code_spec = pl.BlockSpec((1, tall + extra, width), lambda n, *_: (n, 0, 0))
    return pl.pallas_call(
        kernel,
        grid_spec=pltpu.PrefetchScalarGridSpec(
            num_scalar_prefetch=2,
            grid=(tokens // tall,),
            in_specs=[pl.BlockSpec((tall, columns), lambda n, *_: (n, 0))]
            + [part_of(offset) for offset in offsets],
            out_specs=[own_spec if offset == 0 else code_spec for offset in offsets],
        ),
        out_shape=[own if offset == 0 else code for offset in offsets],
        compiler_params=pltpu.CompilerParams(vmem_limit_bytes=60 * 2**20),
        interpret=interpret,
    )(count, mine, grads, *[weight] * len(offsets))


def add_shares(own, shares, interpret=False):
    tokens, width = own.shape
    places = [[(i, j) for i, piece in enumerate(share) for j in range(piece.shape[0])] for share in shares]
    steps = len(places[0])
    tall = tokens // steps
    groups = tall // GROUP
    pieces = [piece for share in shares for piece in share]

    def kernel(own_ref, *refs):
        out, refs = refs[-1], list(refs[:-1])
        held = [[refs.pop(0) for _ in share] for share in shares]
        for step in range(steps):
            blocks = [mine[places[k][step][0]].at[places[k][step][1]] for k, mine in enumerate(held)]
            factors = [
                jnp.exp2(-block[tall : tall + groups, :].astype(jnp.int32).astype(f32))
                for block in blocks
            ]
            for g in range(groups):
                rows = slice(step * tall + g * GROUP, step * tall + (g + 1) * GROUP)
                value = own_ref[rows, :]
                for block, factor in zip(blocks, factors):
                    code = block[g * GROUP : (g + 1) * GROUP, :]
                    value += code.astype(jnp.int32).astype(f32) * factor[g : g + 1]
                out[rows, :] = value.astype(bf16)

    whole = pl.BlockSpec(memory_space=pltpu.VMEM)
    return pl.pallas_call(
        kernel,
        out_shape=jax.ShapeDtypeStruct((tokens, width), bf16),
        in_specs=[whole] * (1 + len(pieces)),
        out_specs=whole,
        compiler_params=pltpu.CompilerParams(vmem_limit_bytes=12 * 2**20),
        interpret=interpret,
    )(own, *pieces)


def place_blocks(pieces, owner_map, me, interpret=False):
    counts = [piece.shape[0] for piece in pieces]
    shape = (sum(counts), *pieces[0].shape[1:])

    def source_slot(position, me):
        core, zh, second, first = position // 32, (position // 16) % 2, (position // 4) % 4, position % 4
        far_x, far_y = (second, first) if zh else (first, second)
        x = lax.rem(lax.div(me, 8) + 4 - far_x, 4)
        y = lax.rem(lax.div(me, 2) + 4 - far_y, 4)
        my_zh, my_core = lax.div(me, 32), lax.rem(me, 2)
        return index_of(1 - my_zh if zh else my_zh, x, y, 1 - my_core if core else my_core)

    def kernel(map_ref, me_ref, *refs):
        sources, out, sent = refs[: len(pieces)], *refs[len(pieces) :]
        at = 0
        for source, count in zip(sources, counts):
            for b in range(count):
                row = map_ref[source_slot(at + b, me_ref[0])]
                pltpu.make_async_copy(source.at[b], out.at[row], sent).start()
            at += count
        pltpu.make_async_copy(out, out, sent).wait()

    return pl.pallas_call(
        kernel,
        out_shape=jax.ShapeDtypeStruct(shape, bf16),
        in_specs=[pl.BlockSpec(memory_space=pltpu.SMEM)] * 2
        + [pl.BlockSpec(memory_space=pltpu.VMEM)] * len(pieces),
        out_specs=pl.BlockSpec(memory_space=pl.ANY),
        scratch_shapes=[pltpu.SemaphoreType.DMA],
        compiler_params=pltpu.CompilerParams(vmem_limit_bytes=12 * 2**20),
        interpret=interpret,
    )(owner_map, me, *pieces)


def per_device(
    hidden_acts, out_grads, token_counts, down_weight, owner_map, master, moment1, moment2
):
    columns = out_grads.shape[1]
    hidden = hidden_acts.shape[1]
    me = lax.axis_index("dp").astype(jnp.int32).reshape(1)
    my_mp = lax.axis_index("mp").astype(jnp.int32).reshape(1)
    ways = lax.axis_size("mp")
    rings = (("x", "y"), ("y", "x"))

    def pass_share(coded, offset):
        ring = [(source, (source + offset) % ways) for source in range(ways)]
        return lax.ppermute(coded, "mp", ring)

    keep, send, up, down = weight_partials(
        hidden_acts, out_grads, down_weight, token_counts, owner_map, me, my_mp, ways
    )
    arrived = to_core(send)
    shares = [[pass_share(up, 1)], [pass_share(down, 3)]]
    arrived, far_grads = lax.optimization_barrier((arrived, out_grads))
    pair = [
        (keep[4 * i : 4 * i + 4].astype(f32) + arrived[4 * i : 4 * i + 4].astype(f32)).astype(bf16)
        for i in range(8)
    ]
    got = [
        [shift(pair[4 * colour + d], first, d) for d in (2, 1, 3)]
        for colour, (first, _) in enumerate(rings)
    ]
    got = lax.optimization_barrier(got)
    across, own = input_shares(far_grads, down_weight, token_counts, my_mp, ways, (2, 0))
    lines = [
        [
            sum((g[e].astype(f32) for g in got[colour]), pair[4 * colour][e].astype(f32)).astype(bf16)
            for e in range(4)
        ]
        for colour in range(2)
    ]
    sums = []
    for line, (_, second) in zip(lines, rings):
        got = lax.optimization_barrier([shift(line[d], second, d) for d in (2, 1, 3)])
        sums.append(sum((g.astype(f32) for g in got), line[0].astype(f32)))
    theirs = to_zh(sums[1])
    summed = sums[0] + theirs

    digits = summed[:1, columns : columns + DIGITS]
    total = jnp.sum(digits * (4.0 ** jnp.arange(DIGITS, dtype=f32)))
    grad = summed[:, :columns] / total
    moment1_new = beta_one * moment1 + (1.0 - beta_one) * grad
    second = beta_two * moment2.astype(f32) + (1.0 - beta_two) * grad * grad
    moment2_new = second.astype(bf16)
    master_new = master - learn_rate * (moment1_new / correct_one) / (
        jnp.sqrt(second / correct_two) + epsilon
    )

    weights = master_new.astype(bf16)[None]
    other = to_zh(weights)
    shares.append([pass_share(across, 2)])
    lines = []
    for part, (first, _) in zip((weights, other), rings):
        two, one, three = [shift(part, first, d) for d in (2, 1, 3)]
        lines.append(jnp.concatenate([part, one, two, three]))
    pieces = []
    for line, (_, second) in zip(lines, rings):
        two, one, three = [shift(line, second, d) for d in (2, 1, 3)]
        pieces += [line, one, two, three]
    pieces += [to_core(piece) for piece in pieces]
    input_grads = add_shares(own, shares)
    weights_new = place_blocks(pieces, owner_map, me).reshape(hidden, columns)
    return (master_new, moment1_new, moment2_new, weights_new, input_grads)


def solution(mesh):
    in_specs = (
        P("dp", None),
        P("dp", "mp"),
        P("dp"),
        P(None, "mp"),
        P(),
        P("dp", "mp"),
        P("dp", "mp"),
        P("dp", "mp"),
    )
    out_specs = (P("dp", "mp"), P("dp", "mp"), P("dp", "mp"), P(None, "mp"), P("dp", "mp"))
    return jax.shard_map(per_device, mesh=mesh, in_specs=in_specs, out_specs=out_specs, check_vma=False)
```

```python
import jax
import jax.numpy as jnp
from jax import lax
from jax.experimental import pallas as pl
from jax.experimental.pallas import tpu as pltpu
from jax.sharding import PartitionSpec as P


beta_one = 0.9
beta_two = 0.95
learn_rate = 0.0003
epsilon = 1e-08
correct_one = 1.0 - 0.9**50
correct_two = 1.0 - 0.95**50


ZH, X, Y, CORE = 2, 4, 4, 2
f32, bf16, i16 = jnp.float32, jnp.bfloat16, jnp.int16
DIGITS = 6
EXTRA = 128
GROUP = 32


def index_of(zh, x, y, core):
    return ((zh * X + x) * Y + y) * CORE + core


def move(value, to):
    pairs = [
        (index_of(z, x, y, c), index_of(*to(z, x, y, c)))
        for z in range(ZH)
        for x in range(X)
        for y in range(Y)
        for c in range(CORE)
    ]
    return lax.ppermute(value, "dp", pairs)


def to_core(value):
    return move(value, lambda z, x, y, c: (z, x, y, 1 - c))


def to_zh(value):
    return move(value, lambda z, x, y, c: (1 - z, x, y, c))


def shift(value, ring, by):
    if ring == "x":
        return move(value, lambda z, x, y, c: (z, (x + by) % X, y, c))
    return move(value, lambda z, x, y, c: (z, x, (y + by) % Y, c))


def relative_slot(position, me):
    core, zh, first, second = position // 32, (position // 16) % 2, (position // 4) % 4, position % 4
    far_x, far_y = (second, first) if zh else (first, second)
    x = lax.rem(lax.div(me, 8) + far_x, 4)
    y = lax.rem(lax.div(me, 2) + far_y, 4)
    my_zh, my_core = lax.div(me, 32), lax.rem(me, 2)
    return index_of(1 - my_zh if zh else my_zh, x, y, 1 - my_core if core else my_core)


def encode(share, out, at):
    tall, width = share.shape
    groups = tall // GROUP
    largest = jnp.max(jnp.abs(share).reshape(groups, GROUP, width), axis=1)
    largest = jnp.max(largest, axis=1, keepdims=True)
    power = jnp.floor(jnp.log2(32000.0 / jnp.maximum(largest, 1e-25)))
    power = jnp.broadcast_to(jnp.minimum(power, 90.0), (groups, width))
    factor = jnp.exp2(power)
    for g in range(groups):
        code = jnp.round(share[g * GROUP : (g + 1) * GROUP] * factor[g : g + 1])
        out[at, g * GROUP : (g + 1) * GROUP, :] = code.astype(jnp.int32).astype(i16)
    out[at, tall : tall + groups, :] = power.astype(jnp.int32).astype(i16)


TALL = 512


def weight_partials(acts, grads, weight, count, owner_map, me, mine, ways, interpret=False):
    tokens, hidden = acts.shape
    columns = grads.shape[1]
    blocks = owner_map.shape[0]
    height = hidden // blocks
    wide = 512
    steps = columns // wide
    near = blocks // 2
    chunk = 512
    parts = tokens // chunk

    width = hidden // ways
    extra = TALL // GROUP

    def kernel(
        count_ref, map_ref, me_ref, mine_ref, acts_ref, grads_ref, up_part_ref, down_part_ref,
        keep_ref, send_ref, up_ref, down_ref, raw, turned, part, up_sum, down_sum, sems,
    ):
        step = pl.program_id(0)

        def add_shares_of(first):
            for weight_ref, total in ((up_part_ref, up_sum), (down_part_ref, down_sum)):
                value = lax.dot_general(
                    grads_ref[...],
                    weight_ref[...],
                    (((1,), (1,)), ((), ())),
                    preferred_element_type=f32,
                )
                total[...] = value if first else total[...] + value

        def put():
            for p in range(blocks):
                start = pl.multiple_of(map_ref[relative_slot(p, me_ref[0])] * height, height)
                out = keep_ref if p < near else send_ref
                out[p % near] = part[pl.ds(start, height), :].astype(bf16)

        @pl.when(step == 0)
        def _():
            loads = [
                pltpu.make_async_copy(
                    acts_ref.at[pl.ds(i * chunk, chunk)], raw.at[pl.ds(i * chunk, chunk)], sems.at[i]
                )
                for i in range(parts)
            ]
            for load in loads:
                load.start()
            for i, load in enumerate(loads):
                rows = pl.ds(i * chunk, chunk)
                load.wait()
                live = lax.broadcasted_iota(jnp.int32, (1, chunk), 1) + i * chunk < count_ref[0]
                flipped = raw[rows, :].T * jnp.where(live, 1.0, 0.0).astype(bf16)
                turned[:, rows] = flipped
                value = jnp.dot(flipped, grads_ref[rows, :], preferred_element_type=f32)
                if i == 0:
                    part[...] = value
                else:
                    part[...] += value
            put()
            add_shares_of(True)

        @pl.when((step > 0) & (step < steps))
        def _():
            part[...] = jnp.dot(turned[...], grads_ref[...], preferred_element_type=f32)
            put()
            add_shares_of(False)

        @pl.when(step == steps)
        def _():
            lane = lax.broadcasted_iota(jnp.int32, (near, height, EXTRA), 2)
            digit = (count_ref[0] >> jnp.minimum(2 * lane, 30)) & 3
            value = digit.astype(f32).astype(bf16)
            keep_ref[:, :, :EXTRA] = value
            send_ref[:, :, :EXTRA] = value
            for i in range(tokens // TALL):
                live = lax.broadcasted_iota(jnp.int32, (TALL, width), 0) + i * TALL < count_ref[0]
                for total, coded_ref in ((up_sum, up_ref), (down_sum, down_ref)):
                    encode(jnp.where(live, total[i * TALL : (i + 1) * TALL], 0.0), coded_ref, i)

    out = jax.ShapeDtypeStruct((near, height, columns + EXTRA), bf16)
    spec = pl.BlockSpec((near, height, wide), lambda n, *_: (0, 0, n))
    code = (tokens // TALL, TALL + extra, width)

    def part_of(offset):
        return pl.BlockSpec(
            (width, wide),
            lambda n, count, map, me, mine: (
                lax.rem(mine[0] + offset, ways),
                jnp.minimum(n, steps - 1),
            ),
        )

    return pl.pallas_call(
        kernel,
        grid_spec=pltpu.PrefetchScalarGridSpec(
            num_scalar_prefetch=4,
            grid=(steps + 1,),
            in_specs=[
                pl.BlockSpec(memory_space=pl.ANY),
                pl.BlockSpec((tokens, wide), lambda n, *_: (0, jnp.minimum(n, steps - 1))),
                part_of(1),
                part_of(ways - 1),
            ],
            out_specs=[spec, spec] + [pl.BlockSpec(code, lambda n, *_: (0, 0, 0))] * 2,
            scratch_shapes=[
                pltpu.VMEM((tokens, hidden), bf16),
                pltpu.VMEM((hidden, tokens), bf16),
                pltpu.VMEM((hidden, wide), f32),
                pltpu.VMEM((tokens, width), f32),
                pltpu.VMEM((tokens, width), f32),
                pltpu.SemaphoreType.DMA((parts,)),
            ],
        ),
        out_shape=[out, out] + [jax.ShapeDtypeStruct(code, i16)] * 2,
        compiler_params=pltpu.CompilerParams(vmem_limit_bytes=60 * 2**20),
        interpret=interpret,
    )(count, owner_map, me, mine, acts, grads, weight, weight)


def far_shares(grads, weight, count, mine, ways, interpret=False):
    tokens, columns = grads.shape
    hidden = weight.shape[0]
    width = hidden // ways
    extra = TALL // GROUP
    steps = tokens // TALL

    def kernel(count_ref, mine_ref, grads_ref, far_ref, near_ref, first_out, rest_out, own_out):
        step = pl.program_id(0)
        live = lax.broadcasted_iota(jnp.int32, (TALL, width), 0) + step * TALL < count_ref[0]

        def share_of(part):
            share = lax.dot_general(
                grads_ref[...], part[...], (((1,), (1,)), ((), ())), preferred_element_type=f32
            )
            return jnp.where(live, share, 0.0)

        @pl.when(step == 0)
        def _():
            encode(share_of(far_ref), first_out, 0)

        @pl.when(step > 0)
        def _():
            encode(share_of(far_ref), rest_out, 0)

        own_out[...] = share_of(near_ref)

    def part_of(offset):
        return pl.BlockSpec(
            (width, columns), lambda n, count, mine: (lax.rem(mine[0] + offset, ways), 0)
        )

    block = (1, TALL + extra, width)
    return pl.pallas_call(
        kernel,
        grid_spec=pltpu.PrefetchScalarGridSpec(
            num_scalar_prefetch=2,
            grid=(steps,),
            in_specs=[pl.BlockSpec((TALL, columns), lambda n, *_: (n, 0)), part_of(2), part_of(0)],
            out_specs=[
                pl.BlockSpec(block, lambda n, *_: (0, 0, 0)),
                pl.BlockSpec(block, lambda n, *_: (jnp.maximum(n - 1, 0), 0, 0)),
                pl.BlockSpec((TALL, width), lambda n, *_: (n, 0)),
            ],
        ),
        out_shape=[
            jax.ShapeDtypeStruct(block, i16),
            jax.ShapeDtypeStruct((steps - 1, *block[1:]), i16),
            jax.ShapeDtypeStruct((tokens, width), f32),
        ],
        compiler_params=pltpu.CompilerParams(vmem_limit_bytes=60 * 2**20),
        interpret=interpret,
    )(count, mine, grads, weight, weight)


def add_shares(own, shares, interpret=False):
    tokens, width = own.shape
    places = [[(i, j) for i, piece in enumerate(share) for j in range(piece.shape[0])] for share in shares]
    steps = len(places[0])
    tall = tokens // steps
    groups = tall // GROUP
    pieces = [piece for share in shares for piece in share]

    def kernel(own_ref, *refs):
        out, refs = refs[-1], list(refs[:-1])
        held = [[refs.pop(0) for _ in share] for share in shares]
        for step in range(steps):
            blocks = [mine[places[k][step][0]].at[places[k][step][1]] for k, mine in enumerate(held)]
            factors = [
                jnp.exp2(-block[tall : tall + groups, :].astype(jnp.int32).astype(f32))
                for block in blocks
            ]
            for g in range(groups):
                rows = slice(step * tall + g * GROUP, step * tall + (g + 1) * GROUP)
                value = own_ref[rows, :]
                for block, factor in zip(blocks, factors):
                    code = block[g * GROUP : (g + 1) * GROUP, :]
                    value += code.astype(jnp.int32).astype(f32) * factor[g : g + 1]
                out[rows, :] = value.astype(bf16)

    whole = pl.BlockSpec(memory_space=pltpu.VMEM)
    return pl.pallas_call(
        kernel,
        out_shape=jax.ShapeDtypeStruct((tokens, width), bf16),
        in_specs=[whole] * (1 + len(pieces)),
        out_specs=whole,
        compiler_params=pltpu.CompilerParams(vmem_limit_bytes=12 * 2**20),
        interpret=interpret,
    )(own, *pieces)


def place_blocks(pieces, owner_map, me, interpret=False):
    counts = [piece.shape[0] for piece in pieces]
    shape = (sum(counts), *pieces[0].shape[1:])

    def source_slot(position, me):
        core, zh, second, first = position // 32, (position // 16) % 2, (position // 4) % 4, position % 4
        far_x, far_y = (second, first) if zh else (first, second)
        x = lax.rem(lax.div(me, 8) + 4 - far_x, 4)
        y = lax.rem(lax.div(me, 2) + 4 - far_y, 4)
        my_zh, my_core = lax.div(me, 32), lax.rem(me, 2)
        return index_of(1 - my_zh if zh else my_zh, x, y, 1 - my_core if core else my_core)

    def kernel(map_ref, me_ref, *refs):
        sources, out, sent = refs[: len(pieces)], *refs[len(pieces) :]
        at = 0
        for source, count in zip(sources, counts):
            for b in range(count):
                row = map_ref[source_slot(at + b, me_ref[0])]
                pltpu.make_async_copy(source.at[b], out.at[row], sent).start()
            at += count
        pltpu.make_async_copy(out, out, sent).wait()

    return pl.pallas_call(
        kernel,
        out_shape=jax.ShapeDtypeStruct(shape, bf16),
        in_specs=[pl.BlockSpec(memory_space=pltpu.SMEM)] * 2
        + [pl.BlockSpec(memory_space=pltpu.VMEM)] * len(pieces),
        out_specs=pl.BlockSpec(memory_space=pl.ANY),
        scratch_shapes=[pltpu.SemaphoreType.DMA],
        compiler_params=pltpu.CompilerParams(vmem_limit_bytes=12 * 2**20),
        interpret=interpret,
    )(owner_map, me, *pieces)


def per_device(
    hidden_acts, out_grads, token_counts, down_weight, owner_map, master, moment1, moment2
):
    columns = out_grads.shape[1]
    hidden = hidden_acts.shape[1]
    me = lax.axis_index("dp").astype(jnp.int32).reshape(1)
    my_mp = lax.axis_index("mp").astype(jnp.int32).reshape(1)
    ways = lax.axis_size("mp")
    rings = (("x", "y"), ("y", "x"))

    def pass_share(coded, offset):
        ring = [(source, (source + offset) % ways) for source in range(ways)]
        return lax.ppermute(coded, "mp", ring)

    keep, send, up, down = weight_partials(
        hidden_acts, out_grads, down_weight, token_counts, owner_map, me, my_mp, ways
    )
    arrived = to_core(send)
    shares = [[pass_share(up, 1)], [pass_share(down, 3)]]
    arrived, far_grads = lax.optimization_barrier((arrived, out_grads))
    pair = [
        (keep[4 * i : 4 * i + 4].astype(f32) + arrived[4 * i : 4 * i + 4].astype(f32)).astype(bf16)
        for i in range(8)
    ]
    got = [
        [shift(pair[4 * colour + d], first, d) for d in (2, 1, 3)]
        for colour, (first, _) in enumerate(rings)
    ]
    got = lax.optimization_barrier(got)
    across_first, across_rest, own = far_shares(
        far_grads, down_weight, token_counts, my_mp, ways
    )
    across_early = pass_share(across_first, 2)
    lines = [
        [
            sum((g[e].astype(f32) for g in got[colour]), pair[4 * colour][e].astype(f32)).astype(bf16)
            for e in range(4)
        ]
        for colour in range(2)
    ]
    sums = []
    for line, (_, second) in zip(lines, rings):
        got = lax.optimization_barrier([shift(line[d], second, d) for d in (2, 1, 3)])
        sums.append(sum((g.astype(f32) for g in got), line[0].astype(f32)))
    theirs = to_zh(sums[1])
    summed = sums[0] + theirs

    digits = summed[:1, columns : columns + DIGITS]
    total = jnp.sum(digits * (4.0 ** jnp.arange(DIGITS, dtype=f32)))
    grad = summed[:, :columns] / total
    moment1_new = beta_one * moment1 + (1.0 - beta_one) * grad
    second = beta_two * moment2.astype(f32) + (1.0 - beta_two) * grad * grad
    moment2_new = second.astype(bf16)
    master_new = master - learn_rate * (moment1_new / correct_one) / (
        jnp.sqrt(second / correct_two) + epsilon
    )

    weights = master_new.astype(bf16)[None]
    other = to_zh(weights)
    shares.append([across_early, pass_share(across_rest, 2)])
    lines = []
    for part, (first, _) in zip((weights, other), rings):
        two, one, three = [shift(part, first, d) for d in (2, 1, 3)]
        lines.append(jnp.concatenate([part, one, two, three]))
    pieces = []
    for line, (_, second) in zip(lines, rings):
        two, one, three = [shift(line, second, d) for d in (2, 1, 3)]
        pieces += [line, one, two, three]
    pieces += [to_core(piece) for piece in pieces]
    weights_new = place_blocks(pieces, owner_map, me).reshape(hidden, columns)
    weights_new, own = lax.optimization_barrier((weights_new, own))
    input_grads = add_shares(own, shares)
    return (master_new, moment1_new, moment2_new, weights_new, input_grads)


def solution(mesh):
    in_specs = (
        P("dp", None),
        P("dp", "mp"),
        P("dp"),
        P(None, "mp"),
        P(),
        P("dp", "mp"),
        P("dp", "mp"),
        P("dp", "mp"),
    )
    out_specs = (P("dp", "mp"), P("dp", "mp"), P("dp", "mp"), P(None, "mp"), P("dp", "mp"))
    return jax.shard_map(per_device, mesh=mesh, in_specs=in_specs, out_specs=out_specs, check_vma=False)
```
